32 devices in a mesh: groups: 2 (over y), ctx: 4 (over z), fsdp: 2 (over x), head: 2 (over core).
Axes of the slice: x: 2, y: 2, z: 4, core: 2. Of those that a mesh axis runs over, the one named last changes fastest.
Arguments:
- hidden_in: bfloat16 [4, 512, 8192], P(('groups', 'fsdp'), 'ctx', 'head'), parts along dimension 0, may hold values from -8 to 8
- w_bc: bfloat16 [8192, 256], P('fsdp'), may hold values from -0.0625 to 0.0625
- x_in: bfloat16 [4, 512, 4096], P(('groups', 'fsdp'), 'ctx', 'head'), parts along dimension 0, may hold values from -6 to 6
- dt_raw: float32 [4, 512, 64], P(('groups', 'fsdp'), 'ctx', 'head'), parts along dimension 0, may hold values from -2 to 5
- decay_rate: float32 [64], P('head'), may hold values from 0.001171875 to 0.033
- conv_x: float32 [4, 4096], P(None, 'head'), may hold values from -3 to 3
- conv_bc: float32 [4, 256], replicated, may hold values from -3 to 3
- skip_gain: float32 [64], P('head'), may hold values from -10 to 10
- span_len: int32 [4, 4], P(('groups', 'fsdp')), parts along dimension 0, may hold values from 1 to 256, 512 in all within a row
- grad_y: bfloat16 [4, 512, 4096], P(('groups', 'fsdp'), 'ctx', 'head'), parts along dimension 0, may hold values from -6 to 6
Outputs:
- grad_x: bfloat16 [4, 512, 4096], P(('groups', 'fsdp'), 'ctx', 'head'), parts along dimension 0
- grad_u: bfloat16 [4, 512, 8192], P(('groups', 'fsdp'), 'ctx', 'head'), parts along dimension 0
- grad_dt: float32 [4, 512, 64], P(('groups', 'fsdp'), 'ctx', 'head'), parts along dimension 0
- grad_w: float32 [4, 4096, 256], P(('groups', 'head'), ('ctx', 'fsdp')), parts along dimension 0
The draws below stay inside these ranges and needn't reach their ends.
There are 2 independent parts, one for each index of `groups`. The reference program is written for one: setup_inputs(seed, part) draws one part's arguments, and reference() takes and returns one part's arrays. A program takes and returns all parts, laid end to end along the dimension named above; an argument that names none is the same for every part. Nothing has to cross between parts.
Inputs may be any that keep to these rules, and one draw needn't show every extreme that they name: `span_len`: each list's spans lie end to end over its 512 tokens; each has 1 to 256 tokens and some span has exactly 256.
All inputs are finite; a program needn't handle non-finite values.
Results may differ from the reference program's by a relative error of at most 0.0057.
Values may be sent and summed in bfloat16 or wider, within the bound.
A program may use at most 128 MiB of HBM per device.

```python
import math
import jax
import jax.numpy as jnp
import numpy as np
from jax import lax

D = 8192
HEADS = 64
HEAD_DIM = 64
STATE = 128
TOK_DEV = 128
INNER = 4096
TOKENS_PER_GROUP = 512
GROUP_COUNT = 2
SPANS = 4
MOST = 256
N_HEAD = 2


def draw_dt_raw(key, part):
    seed_generator, surge_seed_generator = jax.random.split(key)
    ambient_entries = jnp.clip(0.6 * jax.random.normal(seed_generator, (GROUP_COUNT, TOKENS_PER_GROUP, HEADS), jnp.float32) - 0.3, -2.0, 1.0)
    surge_indices = jax.random.randint(surge_seed_generator, (GROUP_COUNT, 8), 0, TOKENS_PER_GROUP)
    surge_amplitudes = jnp.any(jnp.arange(TOKENS_PER_GROUP)[None, :, None] == surge_indices[:, None, :], axis=-1)
    return jnp.where(surge_amplitudes[:, :, None], ambient_entries + 4.0, ambient_entries)


def draw_skip_gain(key, part):
    sign_key, size_key = jax.random.split(jax.random.fold_in(key, 17))
    sign_values = jnp.where(jax.random.bernoulli(sign_key, 0.5, (HEADS,)), 1.0, -1.0).astype(jnp.float32)
    magnitude = jnp.exp(jax.random.uniform(size_key, (HEADS,), jnp.float32, math.log(0.25), math.log(10.0)))
    return sign_values * magnitude


def strengthened(entries, own_key, source, target, parts, factor):
    def block_of(dim):
        return (jnp.arange(entries.shape[dim]) // (entries.shape[dim] // parts)).reshape((-1,) + (1,) * (entries.ndim - 1 - dim))

    near = jax.random.permutation(own_key, parts)[block_of(target)]
    second = (block_of(target) + parts // 2) % parts
    return jnp.where((block_of(source) == near) | (block_of(source) == second), factor * entries, entries)


def steps_of(own_key, extent, cuts, low, high):
    level, own = 1.0, jax.random.fold_in(own_key, 6)
    for dim, parts in cuts:
        steps = jnp.exp(jax.random.uniform(jax.random.fold_in(own, dim), (parts,), jnp.float32, low / len(cuts), high / len(cuts)))
        level = level * jnp.repeat(steps, extent[dim] // parts).reshape([-1 if axis == dim else 1 for axis in range(len(extent))])
    return level


def profile(count, total, limit, slope):
    loads = [(1 << 20) // math.isqrt(rank ** slope) + 1 for rank in range(2, count + 1)]
    rest, given = total - limit - (count - 1), [1] * (count - 1)
    while rest > 0:
        free = [i for i in range(count - 1) if given[i] < limit]
        pool, remaining = sum([loads[i] for i in free]), rest
        for i in free:
            more = min(limit - given[i], max(1, remaining * loads[i] // pool), rest)
            given[i] = given[i] + more
            rest = rest - more
    return np.array([limit] + given)


def ragged(own_key, amount, total, most, lean):
    if amount == 2:
        one = jax.random.randint(own_key, (), max(1, total - most), min(most, total - 1) + 1)
        return jnp.stack([one, total - one])
    sizes = jnp.asarray(profile(amount, total, most, lean), jnp.int32)
    couples = (amount - 1) // 2
    source_of, sink = sizes[1:1 + 2 * couples:2], sizes[2:2 + 2 * couples:2]
    margin = jnp.minimum(source_of - 1, most - sink)
    passed = jax.random.randint(jax.random.fold_in(own_key, 1), (couples,), 0, 1 << 20) % (margin + 1)
    sizes = sizes.at[1:1 + 2 * couples:2].set(source_of - passed).at[2:2 + 2 * couples:2].set(sink + passed)
    return sizes[jax.random.permutation(jax.random.fold_in(own_key, 2), amount)]


def noise(stream_key, extent, spread, reach, shards=(), dtype=jnp.bfloat16):
    values = spread * jax.random.normal(stream_key, extent, jnp.float32)
    if shards:
        values = values * steps_of(stream_key, extent, shards, -0.22, 0.18)
    return jnp.clip(values, -reach, reach).astype(dtype)


def heavy_noise(key, shape, scale, limit, cuts, heavy, kind=jnp.bfloat16):
    entries = scale * jax.random.normal(key, shape, jnp.float32)
    if cuts:
        entries = entries * steps_of(key, shape, cuts, -0.22, 0.18)
    return jnp.clip(strengthened(entries, jax.random.fold_in(key, 3), *heavy), -limit, limit).astype(kind)


def setup_inputs(seed: int = 0, part: int = 0) -> dict:
    keys = jax.random.split(jax.random.key(seed), 11)
    own_keys = jax.random.split(jax.random.fold_in(keys[10], part), 11)
    return {
        "hidden_in": heavy_noise(own_keys[0], (GROUP_COUNT, TOKENS_PER_GROUP, D), 1.0, 8.0, ((0, 2), (1, 4), (2, 2)), (1, 2, 4, 2.0)),
        "w_bc": noise(keys[1], (D, 2 * STATE), D ** -0.5, 0.0625, ((0, 2),)),
        "x_in": noise(own_keys[2], (GROUP_COUNT, TOKENS_PER_GROUP, INNER), 1.0, 6.0, ((0, 2), (1, 4), (2, 2))),
        "dt_raw": draw_dt_raw(jax.random.fold_in(jax.random.fold_in(keys[10], part), 71), part),
        "decay_rate": jnp.clip(jnp.exp(math.log(0.033) - 3.3379025 * jax.random.uniform(keys[4], (HEADS,), jnp.float32) ** steps_of(keys[4], (HEADS,), ((0, 2),), -0.2, 0.2)), 0.001171875, 0.033),
        "conv_x": noise(keys[5], (4, INNER), 0.5, 3.0, ((1, 2),), jnp.float32),
        "conv_bc": noise(keys[6], (4, 2 * STATE), 0.5, 3.0, (), jnp.float32),
        "skip_gain": draw_skip_gain(jax.random.fold_in(keys[10], 71), part),
        "span_len": jax.vmap(lambda own: ragged(own, SPANS, TOKENS_PER_GROUP, MOST, 1))(jax.random.split(own_keys[8], GROUP_COUNT)).reshape((GROUP_COUNT, SPANS)).astype(jnp.int32),
        "grad_y": noise(own_keys[9], (GROUP_COUNT, TOKENS_PER_GROUP, INNER), 1.0, 6.0, ((0, 2), (1, 4), (2, 2))),
    }


exact_mode = lax.Precision.HIGHEST

def causal_conv(values, conv_taps, segment):
    tok_rows = values.shape[0] - 3
    summed = jnp.zeros((tok_rows, values.shape[1]), jnp.float32)
    for offset in range(4):
        same_span = (segment[offset:offset + tok_rows] == segment[3:]).astype(jnp.float32)
        summed = summed + conv_taps[offset][None, :] * values[offset:offset + tok_rows] * same_span[:, None]
    return summed

def prepare(x_halo, bc_halo, raw_steps, segment, conv_x, conv_bc, decay_rate):
    x_conv = jax.nn.silu(causal_conv(x_halo, conv_x, segment))
    bc_conv = jax.nn.silu(causal_conv(bc_halo, conv_bc, segment))
    dt_soft = jax.nn.softplus(raw_steps)
    log_step = -dt_soft * decay_rate[None, :]
    return (x_conv, bc_conv[:, :STATE], bc_conv[:, STATE:], dt_soft, log_step)

def block_outputs(x_conv, b_state, c_state, dt_soft, log_step, start_state, segment, seg_before, skip_gain):
    tok_rows = x_conv.shape[0]
    head_count = dt_soft.shape[1]
    x_heads = x_conv.reshape(tok_rows, head_count, -1)
    cumulative = jnp.cumsum(log_step, axis=0).T
    token_index = jnp.arange(tok_rows)
    within = (segment[:, None] == segment[None, :]) & (token_index[:, None] >= token_index[None, :])
    log_gap = cumulative[:, :, None] - cumulative[:, None, :]
    decay_table = jnp.where(within[None], jnp.exp(jnp.where(within[None], log_gap, 0.0)), 0.0)
    scores = jnp.dot(c_state, b_state.T, precision=exact_mode, preferred_element_type=jnp.float32)
    weighted = x_heads * dt_soft[:, :, None]
    intra_out = jnp.einsum('hts,shp->thp', decay_table * scores[None], weighted, precision=exact_mode)
    alive_mask = (segment == seg_before).astype(jnp.float32)
    carried = jnp.exp(cumulative.T) * alive_mask[:, None]
    state_out = jnp.einsum('tn,hpn->thp', c_state, start_state, precision=exact_mode) * carried[:, :, None]
    result = intra_out + state_out + skip_gain[None, :, None] * x_heads
    return result.reshape(tok_rows, -1)

def block_ends(x_conv, b_state, dt_soft, log_step, segment, seg_before):
    tok_rows = x_conv.shape[0]
    head_count = dt_soft.shape[1]
    x_heads = x_conv.reshape(tok_rows, head_count, -1)
    cumulative = jnp.cumsum(log_step, axis=0)
    last_same = (segment == segment[-1]).astype(jnp.float32)
    toward = jnp.exp(cumulative[-1][None, :] - cumulative) * last_same[:, None]
    weighted = x_heads * (dt_soft * toward)[:, :, None]
    ends_state = jnp.einsum('shp,sn->hpn', weighted, b_state, precision=exact_mode)
    through = jnp.exp(cumulative[-1]) * (segment[-1] == seg_before).astype(jnp.float32)
    return (through, ends_state)

def reference(hidden_in, w_bc, x_in, dt_raw, decay_rate, conv_x, conv_bc, skip_gain, span_len, grad_y):
    blocks = TOKENS_PER_GROUP // TOK_DEV

    def one_list(grad_w, list_items):
        hidden, x_list, raw_list, lengths, cotangent = list_items
        span_ends = jnp.cumsum(lengths)
        position = jnp.arange(TOKENS_PER_GROUP)
        segment = lax.optimization_barrier(jnp.sum((span_ends[None, :] <= position[:, None]).astype(jnp.int32), axis=1)).astype(jnp.int32)
        padded_seg = jnp.concatenate([jnp.full((3,), -1, jnp.int32), segment])
        bc_pre = jnp.dot(hidden, w_bc, preferred_element_type=jnp.float32).astype(jnp.bfloat16)
        befores = padded_seg[2:2 + TOKENS_PER_GROUP:TOK_DEV]

        def forward(x_vals, bc_vals, raw_vals):
            x_halo = jnp.concatenate([jnp.zeros((3, INNER), jnp.float32), x_vals])
            bc_halo = jnp.concatenate([jnp.zeros((3, 2 * STATE), jnp.float32), bc_vals])
            x_conv, b_state, c_state, dt_soft, log_step = prepare(x_halo, bc_halo, raw_vals, padded_seg, conv_x, conv_bc, decay_rate)

            def block_step(carry_state, block_items):
                x_block, b_block, c_block, dt_block, log_block, seg_block, before = block_items
                result = block_outputs(x_block, b_block, c_block, dt_block, log_block, carry_state, seg_block, before, skip_gain)
                through, ends_state = block_ends(x_block, b_block, dt_block, log_block, seg_block, before)
                return (through[:, None, None] * carry_state + ends_state, result)
            block_items = (x_conv.reshape(blocks, TOK_DEV, INNER), b_state.reshape(blocks, TOK_DEV, STATE), c_state.reshape(blocks, TOK_DEV, STATE), dt_soft.reshape(blocks, TOK_DEV, HEADS), log_step.reshape(blocks, TOK_DEV, HEADS), segment.reshape(blocks, TOK_DEV), befores)
            start = jnp.zeros((HEADS, HEAD_DIM, STATE), jnp.float32)
            unused, outputs = lax.scan(block_step, start, block_items)
            return outputs.reshape(TOKENS_PER_GROUP, INNER)
        unused, pullback = jax.vjp(forward, x_list.astype(jnp.float32), bc_pre.astype(jnp.float32), raw_list)
        grad_xin, d_bcpre, grad_raw = pullback(cotangent.astype(jnp.float32))
        d_bc = d_bcpre.astype(jnp.bfloat16)
        grad_hidden = jnp.dot(d_bc, w_bc.T, preferred_element_type=jnp.float32).astype(jnp.bfloat16)
        grad_w = grad_w + lax.dot_general(hidden, d_bc, (((0,), (0,)), ((), ())), preferred_element_type=jnp.float32)
        return (grad_w, (grad_xin.astype(jnp.bfloat16), grad_hidden, grad_raw))
    start_w = jnp.zeros((D, 2 * STATE), jnp.float32)
    grad_w, stacked = lax.scan(one_list, start_w, (hidden_in, x_in, dt_raw, span_len, grad_y))
    grad_x, grad_u, grad_dt = stacked
    return (grad_x, grad_u, grad_dt, grad_w.reshape(N_HEAD, D // N_HEAD, 2 * STATE))
```

```python
import jax
import jax.numpy as jnp
from jax import lax
from jax.experimental import pallas as pl
from jax.experimental.pallas import tpu as pltpu
from jax.sharding import PartitionSpec as P

STATE = 128
HEAD = 64
MOST = 256
BF = jnp.bfloat16
F32 = jnp.float32
EXACT = lax.Precision.HIGHEST


def shifted(block, axis, distance):
    devices = range(lax.axis_size(axis))
    route = [(i - distance, i) for i in devices if i - distance in devices]
    return lax.ppermute(block, axis, route)


def dot(a, b, ca, cb, precision=None):
    return lax.dot_general(
        a, b, (((ca,), (cb,)), ((), ())), precision=precision, preferred_element_type=F32
    )


def ssm_kernel(
    x2, x1, x0, g0, g1, g2, b2, b1, b0, b3, b4, raw_ref, info_ref, segrow_ref,
    decay_ref, skip_ref, tapx_ref, tapb_ref,
    dx_ref, tail_ref, rim_ref, dbc_ref, rimbc_ref, ddt_ref,
    masks, bias_ref, s_ref, cols_a, cols_b, cum_rows, bprev, cnext, bown, cown,
    silu_bc, d_s, d_b, d_c, acc,
):
    T = x0.shape[0]
    pairs = x0.shape[1] // 128
    lane = lax.broadcasted_iota(jnp.int32, (T, 128), 1)
    row = lax.broadcasted_iota(jnp.int32, (T, 128), 0)
    low = lane < HEAD
    group = lane // 32
    info = info_ref[...]
    for k in range(3):
        masks[k] = jnp.broadcast_to(info[: 3 * T, k : k + 1], (3 * T, 128))

    def col(block, k):
        return info[block * T : (block + 1) * T, k : k + 1]

    tri = (row >= lane).astype(F32)
    decay = decay_ref[...]
    dts, cums, carried, toward = [], [], [], []
    for j in range(5):
        raw = raw_ref[j * T : (j + 1) * T, :]
        dt = jnp.maximum(raw, 0.0) + jnp.log1p(jnp.exp(-jnp.abs(raw)))
        cum = dot(tri, -dt * decay, 1, 0, EXACT)
        dts.append(dt)
        cums.append(cum)
        carried.append(jnp.exp(cum) * col(j, 3))
        toward.append(jnp.exp(cum[T - 1 :, :] - cum) * col(j, 4))
    a1 = dts[1] * toward[1]
    a2 = dts[0] * toward[0] * carried[1][T - 1 :, :]
    c1 = carried[3]
    c2 = carried[4] * carried[3][T - 1 :, :]

    def packed(p, q, r, s):
        return jnp.where(group == 0, p, jnp.where(group == 1, q, jnp.where(group == 2, r, s)))

    cols_a[...] = packed(dts[2], cums[2], carried[2], toward[2])
    cols_b[...] = packed(a2, a1, c1, c2)
    cum_rows[...] = cums[2].T
    same = col(2, 5) == segrow_ref[...]
    bias_ref[...] = jnp.where(same & (row >= lane), 0.0, -1e30)

    taps_b = tapb_ref[...]
    bc = jnp.concatenate([b2[...], b1[...], b0[...], b3[...], b4[...]]).astype(F32)
    pre_bc = taps_b[3:4, :] * bc
    for k in range(3):
        pre_bc += taps_b[k : k + 1, :] * pltpu.roll(bc, 3 - k, 0) * info[:, k : k + 1]
    sig_bc = jax.nn.sigmoid(pre_bc)
    conv_bc = pre_bc * sig_bc
    own_sig = sig_bc[2 * T : 3 * T]
    silu_bc[...] = own_sig * (1.0 + pre_bc[2 * T : 3 * T] * (1.0 - own_sig))
    bprev[...] = conv_bc[: 2 * T, :STATE].astype(BF)
    cnext[...] = conv_bc[3 * T :, STATE:].astype(BF)
    bown[...] = conv_bc[2 * T : 3 * T, :STATE]
    cown[...] = conv_bc[2 * T : 3 * T, STATE:]
    s_ref[...] = dot(cown[...], bown[...], 1, 1, EXACT)
    d_s[...] = jnp.zeros_like(d_s)
    d_b[...] = jnp.zeros_like(d_b)
    d_c[...] = jnp.zeros_like(d_c)
    acc[...] = jnp.zeros_like(acc)

    def pair(i, carry):
        at = pl.ds(pl.multiple_of(i * 128, 128), 128)
        ca = pltpu.roll(cols_a[...], (128 - 2 * i) % 128, 1)
        cb = pltpu.roll(cols_b[...], (128 - 2 * i) % 128, 1)

        def wide(c, q):
            return jnp.where(low, c[:, 32 * q : 32 * q + 1], c[:, 32 * q + 1 : 32 * q + 2])

        def tall(c, q):
            return c[:, 32 * q : 32 * q + 1], c[:, 32 * q + 1 : 32 * q + 2]

        taps = tapx_ref[:, at]
        xe = jnp.concatenate([x2[:, at], x1[:, at], x0[:, at]]).astype(F32)
        pre = taps[3:4, :] * xe
        for k in range(3):
            pre += taps[k : k + 1, :] * pltpu.roll(xe, 3 - k, 0) * masks[k]
        sig = jax.nn.sigmoid(pre)
        xc = pre * sig
        xown = xc[2 * T :]
        sown = sig[2 * T :]
        dsilu = sown * (1.0 + pre[2 * T :] * (1.0 - sown))
        dt_w = wide(ca, 0)
        toward_w = wide(ca, 3)
        xw = jnp.concatenate([xc[:T] * wide(cb, 0), xc[T : 2 * T] * wide(cb, 1)]).astype(BF)
        start = dot(xw, bprev[...], 0, 0)
        gw = jnp.concatenate(
            [g1[:, at].astype(F32) * wide(cb, 2), g2[:, at].astype(F32) * wide(cb, 3)]
        ).astype(BF)
        end_grad = dot(gw, cnext[...], 0, 0)
        start_b = start.astype(BF)
        end_b = end_grad.astype(BF)
        gy = g0[:, at].astype(F32)
        gg = jnp.concatenate([jnp.where(low, gy, 0.0), jnp.where(low, 0.0, gy)]).astype(BF)
        xt = xown * dt_w
        xt_b = xt.astype(BF)
        xx = jnp.concatenate([jnp.where(low, xt, 0.0), jnp.where(low, 0.0, xt)]).astype(BF)
        d_m = dot(gg, xt_b, 1, 1)
        cum_a, cum_b = tall(ca, 1)
        bias = bias_ref[...]
        decay_t = jnp.concatenate(
            [
                jnp.exp(cum_a - cum_rows[pl.ds(2 * i, 1), :] + bias),
                jnp.exp(cum_b - cum_rows[pl.ds(2 * i + 1, 1), :] + bias),
            ]
        )
        s_all = s_ref[...]
        s_two = jnp.concatenate([s_all, s_all])
        ls = decay_t * s_two
        ldm = decay_t * d_m
        d_s[...] += ldm[:T] + ldm[T:]
        d_x = dot(ls.astype(BF), gg, 0, 0)
        car = jnp.concatenate(tall(ca, 2))
        tow = jnp.concatenate(tall(ca, 3))
        c_u = car * dot(gg, start_b, 1, 0)
        d_c[...] += c_u[:T] + c_u[T:]
        c_own = cown[...]
        c_two = jnp.concatenate([c_own, c_own])
        r = jnp.sum(ldm * s_two + c_u * c_two, axis=1, keepdims=True)
        t_v = tow * dot(xx, end_b, 1, 0)
        d_b[...] += t_v[:T] + t_v[T:]
        d_xe = dot(bown[...].astype(BF), end_b, 1, 1) * toward_w
        d_xt = d_x + d_xe
        prod = xown * d_xt
        q_a = jnp.sum(jnp.where(low, prod, 0.0), axis=1, keepdims=True)
        q_b = jnp.sum(jnp.where(low, 0.0, prod), axis=1, keepdims=True)
        ends = jnp.sum(xt * d_xe, axis=0, keepdims=True)
        inner = end_grad * start
        low_row = low[:1]
        through_a, through_b = (v[T - 1 :, :] for v in tall(ca, 2))
        last_a = jnp.sum(jnp.where(low_row, ends, 0.0), axis=1, keepdims=True) + through_a * jnp.sum(
            jnp.sum(inner[:HEAD], axis=0, keepdims=True), axis=1, keepdims=True
        )
        last_b = jnp.sum(jnp.where(low_row, 0.0, ends), axis=1, keepdims=True) + through_b * jnp.sum(
            jnp.sum(inner[HEAD:], axis=0, keepdims=True), axis=1, keepdims=True
        )
        dt_a, dt_b = tall(ca, 0)
        final = row[:, :1] == T - 1
        cum_ga = r[:T] - dt_a * q_a + jnp.where(final, last_a, 0.0)
        cum_gb = r[T:] - dt_b * q_b + jnp.where(final, last_b, 0.0)
        placed = jnp.where(
            lane == 0,
            q_a,
            jnp.where(
                lane == 1, q_b, jnp.where(lane == 32, cum_ga, jnp.where(lane == 33, cum_gb, 0.0))
            ),
        )
        acc[...] += pltpu.roll(placed, 2 * i, 1)
        d_pre = (dt_w * d_xt + skip_ref[:, at] * gy) * dsilu
        own = taps[3:4, :] * d_pre
        rim = jnp.zeros((8, 128), F32)
        for k in range(3):
            d = 3 - k
            z = pltpu.roll(taps[k : k + 1, :] * masks[k, 2 * T :] * d_pre, T - d, 0)
            own += jnp.where(row < T - d, z, 0.0)
            rim += jnp.where(row[T - 8 :] < T - d, 0.0, z[T - 8 :])
        dx_ref[:, at] = own.astype(BF)
        tail_ref[:, at] = own[T - 8 :]
        rim_ref[:, at] = rim
        return carry

    lax.fori_loop(0, pairs, pair, 0)

    ds = d_s[...]
    full_c = d_c[...] + dot(ds, bown[...], 1, 0, EXACT)
    full_b = d_b[...] + dot(ds, cown[...], 0, 0, EXACT)
    d_pre = jnp.concatenate([full_b, full_c], axis=1) * silu_bc[...]
    own = taps_b[3:4, :] * d_pre
    rim = jnp.zeros((8, 2 * STATE), F32)
    row2 = lax.broadcasted_iota(jnp.int32, (T, 2 * STATE), 0)
    for k in range(3):
        d = 3 - k
        z = pltpu.roll(taps_b[k : k + 1, :] * info[2 * T : 3 * T, k : k + 1] * d_pre, T - d, 0)
        own += jnp.where(row2 < T - d, z, 0.0)
        rim += jnp.where(row2[T - 8 :] < T - d, 0.0, z[T - 8 :])
    dbc_ref[...] = own
    rimbc_ref[...] = rim
    total = acc[...]
    d_log = pltpu.roll(dot(tri, total, 0, 0, EXACT), 96, 1)
    raw = raw_ref[2 * T : 3 * T, :]
    ddt_ref[...] = ((total - decay * d_log) * jax.nn.sigmoid(raw))[:, :32]


def ssm(xs, gs, bcs, raw, info, segrow, decay, skip, tapx, tapb):
    T, W = xs[0].shape
    vm = pltpu.VMEM
    return pl.pallas_call(
        ssm_kernel,
        out_shape=(
            jax.ShapeDtypeStruct((T, W), BF),
            jax.ShapeDtypeStruct((8, W), F32),
            jax.ShapeDtypeStruct((8, W), F32),
            jax.ShapeDtypeStruct((T, 2 * STATE), F32),
            jax.ShapeDtypeStruct((8, 2 * STATE), F32),
            jax.ShapeDtypeStruct((T, 32), F32),
        ),
        scratch_shapes=[
            vm((3, 3 * T, 128), F32), vm((T, T), F32), vm((T, T), F32), vm((T, 128), F32),
            vm((T, 128), F32), vm((128, T), F32), vm((2 * T, STATE), BF), vm((2 * T, STATE), BF),
            vm((T, STATE), F32), vm((T, STATE), F32), vm((T, 2 * STATE), F32),
            vm((T, T), F32), vm((T, STATE), F32), vm((T, STATE), F32), vm((T, 128), F32),
        ],
        compiler_params=pltpu.CompilerParams(vmem_limit_bytes=40 << 20),
        cost_estimate=pl.CostEstimate(
            flops=2 * 9 * T * 256 * W, bytes_accessed=8 * T * W * 2, transcendentals=6 * T * W
        ),
    )(*xs, *gs, *bcs, raw, info, segrow, decay, skip, tapx, tapb)


def on_device(
    hidden_in, w_bc, x_in, dt_raw, decay_rate, conv_x, conv_bc, skip_gain, span_len, grad_y
):
    T = x_in.shape[1]
    hidden = hidden_in[0]
    half_width = hidden.shape[1]
    n_ctx, n_fsdp, n_head = (lax.axis_size(a) for a in ("ctx", "fsdp", "head"))
    assert T * 2 == MOST and dt_raw.shape[2] == 32
    x0, g0, raw0 = x_in[0], grad_y[0], dt_raw[0]
    if n_fsdp == n_head:
        route = [(f * n_head + h, h * n_head + f) for f in range(n_fsdp) for h in range(n_head)]
        w_half = lax.ppermute(w_bc, ("fsdp", "head"), route)
    else:
        w_full = lax.all_gather(w_bc, "fsdp", axis=0, tiled=True)
        w_half = lax.dynamic_slice_in_dim(
            w_full, lax.axis_index("head") * half_width, half_width, 0
        )
    raws = [shifted(raw0, "ctx", d) for d in (2, 1)] + [raw0] + [shifted(raw0, "ctx", -d) for d in (1, 2)]
    x1, g1 = shifted(x0, "ctx", 1), shifted(g0, "ctx", -1)
    x2, g2 = shifted(x0, "ctx", 2), shifted(g0, "ctx", -2)

    swap = [(i, (i + 1) % n_head) for i in range(n_head)]
    partial_bc = jnp.dot(hidden, w_half, preferred_element_type=F32)
    bc_pre = (partial_bc + lax.ppermute(partial_bc, "head", swap)).astype(BF)
    bcs = [shifted(bc_pre, "ctx", d) for d in (2, 1)] + [bc_pre] + [shifted(bc_pre, "ctx", -d) for d in (1, 2)]

    n_blocks = n_ctx * n_fsdp
    blocks = hidden.reshape(T, n_blocks, half_width // n_blocks).transpose(1, 0, 2)
    hidden_all = lax.all_to_all(blocks, ("ctx", "fsdp"), 0, 0, tiled=True)

    position = (lax.axis_index("ctx") - 2) * T + jnp.arange(-3, 5 * T, dtype=jnp.int32)
    span_ends = jnp.cumsum(span_len[0])
    counted = jnp.sum((span_ends[None, :] <= position[:, None]).astype(jnp.int32), axis=1)
    segment = jnp.where(position >= 0, counted, -1).astype(F32)
    own_seg = segment[3:]
    by_block = own_seg.reshape(5, T)
    before = jnp.broadcast_to(segment[2 : 2 + 5 * T : T][:, None], (5, T)).reshape(-1)
    last = jnp.broadcast_to(by_block[:, T - 1 :], (5, T)).reshape(-1)
    info = jnp.stack(
        [(segment[k : k + 5 * T] == own_seg).astype(F32) for k in range(3)]
        + [(own_seg == before).astype(F32), (own_seg == last).astype(F32), own_seg],
        axis=1,
    )
    segrow = by_block[2:3]
    raw = jnp.tile(jnp.concatenate(raws), (1, 4))
    decay = jnp.tile(decay_rate, 4)[None, :]
    skip = jnp.repeat(skip_gain, HEAD)[None, :]

    dx, tail, rim, dbc, rimbc, ddt = ssm(
        (x2, x1, x0), (g0, g1, g2), bcs, raw, info, segrow, decay, skip, conv_x, conv_bc
    )
    back = shifted(rim, "ctx", -1)
    grad_x = lax.dynamic_update_slice(dx, (tail + back).astype(BF), (T - 8, 0))

    other = lax.ppermute(dbc, "head", swap)
    rim_same = shifted(rimbc, "ctx", -1)
    cross = [
        (c * n_head + h, (c - 1) * n_head + (h + 1) % n_head)
        for c in range(1, n_ctx)
        for h in range(n_head)
    ]
    rim_cross = lax.ppermute(rimbc, ("ctx", "head"), cross)
    d_bc = ((dbc + other) + jnp.pad(rim_same + rim_cross, ((T - 8, 0), (0, 0)))).astype(BF)
    grad_u = lax.dot_general(
        d_bc, w_half, (((1,), (1,)), ((), ())), preferred_element_type=F32
    ).astype(BF)
    d_all = lax.all_gather(d_bc, ("ctx", "fsdp"), axis=0)
    grad_w = lax.dot_general(
        hidden_all.reshape(n_blocks * T, -1),
        d_all.reshape(n_blocks * T, -1),
        (((0,), (0,)), ((), ())),
        preferred_element_type=F32,
    )
    return (grad_x[None], grad_u[None], ddt[None], grad_w[None])


def solution(mesh):
    return jax.shard_map(
        on_device,
        mesh=mesh,
        in_specs=(
            P(("groups", "fsdp"), "ctx", "head"),
            P("fsdp", None),
            P(("groups", "fsdp"), "ctx", "head"),
            P(("groups", "fsdp"), "ctx", "head"),
            P("head"),
            P(None, "head"),
            P(),
            P("head"),
            P(("groups", "fsdp"), None),
            P(("groups", "fsdp"), "ctx", "head"),
        ),
        out_specs=(
            P(("groups", "fsdp"), "ctx", "head"),
            P(("groups", "fsdp"), "ctx", "head"),
            P(("groups", "fsdp"), "ctx", "head"),
            P(("groups", "head"), ("ctx", "fsdp"), None),
        ),
        check_vma=False,
    )
```

```python
import jax
import jax.numpy as jnp
from jax import lax
from jax.experimental import pallas as pl
from jax.experimental.pallas import tpu as pltpu
from jax.sharding import PartitionSpec as P

STATE = 128
HEAD = 64
MOST = 256
BF = jnp.bfloat16
F32 = jnp.float32
EXACT = lax.Precision.HIGHEST


def shifted(block, axis, distance):
    devices = range(lax.axis_size(axis))
    route = [(i - distance, i) for i in devices if i - distance in devices]
    return lax.ppermute(block, axis, route)


def dot(a, b, ca, cb, precision=None):
    return lax.dot_general(
        a, b, (((ca,), (cb,)), ((), ())), precision=precision, preferred_element_type=F32
    )


def ssm_setup(T, c, span_ref, masks, bias_ref):
    spans = span_ref.shape[1]
    ends, total = [], 0
    for i in range(spans):
        total = total + span_ref[0, i]
        ends.append(total)

    def segment(p):
        count = sum((e <= p).astype(jnp.int32) if hasattr(p, "shape") and p.shape else jnp.where(e <= p, 1, 0) for e in ends)
        return jnp.where(p >= 0, count, -1)

    iota = lax.broadcasted_iota(jnp.int32, (T, 1), 0)
    taps, alive, last_same = [[], [], []], [], []
    for j in range(5):
        base = (c - 2 + j) * T
        pos = base + iota
        own = segment(pos)
        for k in range(3):
            taps[k].append((segment(pos - 3 + k) == own).astype(F32))
        alive.append((own == segment(base - 1)).astype(F32))
        last_same.append((own == segment(base + T - 1)).astype(F32))
    for k in range(3):
        masks[k] = jnp.broadcast_to(jnp.concatenate(taps[k][:3]), (3 * T, 128))
    row_pos = c * T + lax.broadcasted_iota(jnp.int32, (1, T), 1)
    same = segment(c * T + iota) == segment(row_pos)
    row = lax.broadcasted_iota(jnp.int32, (T, T), 0)
    lane = lax.broadcasted_iota(jnp.int32, (T, T), 1)
    bias_ref[...] = jnp.where(same & (row >= lane), 0.0, -1e30)
    return [jnp.concatenate(t) for t in taps], alive, last_same


def ssm_body(
    setup, x2, x1, x0, g0, g1, g2, b2, b1, b0, b3, b4, raw_ref,
    decay_ref, skip_ref, tapx_ref, tapb_ref,
    dx_ref, tail_ref, rim_ref, dbc_ref, rimbc_ref, ddt_ref,
    masks, bias_ref, s_ref, cols_a, cols_b, cum_rows, bprev, cnext, bown, cown,
    silu_bc, d_s, d_b, d_c, acc,
):
    T = x0.shape[0]
    pairs = x0.shape[1] // 128
    lane = lax.broadcasted_iota(jnp.int32, (T, 128), 1)
    row = lax.broadcasted_iota(jnp.int32, (T, 128), 0)
    low = lane < HEAD
    group = lane // 32
    tap_masks, alive, last_same = setup
    tri = (row >= lane).astype(F32)
    decay = jnp.concatenate([decay_ref[...]] * 4, axis=1)
    dts, cums, carried, toward = [], [], [], []
    for j in range(5):
        raw = raw_ref[j]
        dt = jnp.maximum(raw, 0.0) + jnp.log1p(jnp.exp(-jnp.abs(raw)))
        cum = dot(tri, -dt * decay, 1, 0, EXACT)
        dts.append(dt)
        cums.append(cum)
        carried.append(jnp.exp(cum) * alive[j])
        toward.append(jnp.exp(cum[T - 1 :, :] - cum) * last_same[j])
    a1 = dts[1] * toward[1]
    a2 = dts[0] * toward[0] * carried[1][T - 1 :, :]
    c1 = carried[3]
    c2 = carried[4] * carried[3][T - 1 :, :]

    def packed(p, q, r, s):
        return jnp.where(group == 0, p, jnp.where(group == 1, q, jnp.where(group == 2, r, s)))

    cols_a[...] = packed(dts[2], cums[2], carried[2], toward[2])
    cols_b[...] = packed(a2, a1, c1, c2)
    cum_rows[...] = cums[2].T

    taps_b = tapb_ref[...]
    bc = jnp.concatenate([b2[...], b1[...], b0[...], b3[...], b4[...]]).astype(F32)
    pre_bc = taps_b[3:4, :] * bc
    for k in range(3):
        pre_bc += taps_b[k : k + 1, :] * pltpu.roll(bc, 3 - k, 0) * tap_masks[k]
    sig_bc = jax.nn.sigmoid(pre_bc)
    conv_bc = pre_bc * sig_bc
    own_sig = sig_bc[2 * T : 3 * T]
    silu_bc[...] = own_sig * (1.0 + pre_bc[2 * T : 3 * T] * (1.0 - own_sig))
    bprev[...] = conv_bc[: 2 * T, :STATE].astype(BF)
    cnext[...] = conv_bc[3 * T :, STATE:].astype(BF)
    bown[...] = conv_bc[2 * T : 3 * T, :STATE]
    cown[...] = conv_bc[2 * T : 3 * T, STATE:]
    s_ref[...] = dot(cown[...], bown[...], 1, 1, EXACT)
    d_s[...] = jnp.zeros_like(d_s)
    d_b[...] = jnp.zeros_like(d_b)
    d_c[...] = jnp.zeros_like(d_c)
    acc[...] = jnp.zeros_like(acc)

    def pair(i, carry):
        at = pl.ds(pl.multiple_of(i * 128, 128), 128)
        ca = pltpu.roll(cols_a[...], (128 - 2 * i) % 128, 1)
        cb = pltpu.roll(cols_b[...], (128 - 2 * i) % 128, 1)

        def wide(c, q):
            return jnp.where(low, c[:, 32 * q : 32 * q + 1], c[:, 32 * q + 1 : 32 * q + 2])

        def tall(c, q):
            return c[:, 32 * q : 32 * q + 1], c[:, 32 * q + 1 : 32 * q + 2]

        taps = tapx_ref[:, at]
        xe = jnp.concatenate([x2[:, at], x1[:, at], x0[:, at]]).astype(F32)
        pre = taps[3:4, :] * xe
        for k in range(3):
            pre += taps[k : k + 1, :] * pltpu.roll(xe, 3 - k, 0) * masks[k]
        sig = jax.nn.sigmoid(pre)
        xc = pre * sig
        xown = xc[2 * T :]
        sown = sig[2 * T :]
        dsilu = sown * (1.0 + pre[2 * T :] * (1.0 - sown))
        dt_w = wide(ca, 0)
        toward_w = wide(ca, 3)
        xw = jnp.concatenate([xc[:T] * wide(cb, 0), xc[T : 2 * T] * wide(cb, 1)]).astype(BF)
        start = dot(xw, bprev[...], 0, 0)
        gw = jnp.concatenate(
            [g1[:, at].astype(F32) * wide(cb, 2), g2[:, at].astype(F32) * wide(cb, 3)]
        ).astype(BF)
        end_grad = dot(gw, cnext[...], 0, 0)
        start_b = start.astype(BF)
        end_b = end_grad.astype(BF)
        gy = g0[:, at].astype(F32)
        gg = jnp.concatenate([jnp.where(low, gy, 0.0), jnp.where(low, 0.0, gy)]).astype(BF)
        xt = xown * dt_w
        xt_b = xt.astype(BF)
        xx = jnp.concatenate([jnp.where(low, xt, 0.0), jnp.where(low, 0.0, xt)]).astype(BF)
        d_m = dot(gg, xt_b, 1, 1)
        cum_a, cum_b = tall(ca, 1)
        bias = bias_ref[...]
        decay_t = jnp.concatenate(
            [
                jnp.exp(cum_a - cum_rows[pl.ds(2 * i, 1), :] + bias),
                jnp.exp(cum_b - cum_rows[pl.ds(2 * i + 1, 1), :] + bias),
            ]
        )
        s_all = s_ref[...]
        s_two = jnp.concatenate([s_all, s_all])
        ls = decay_t * s_two
        ldm = decay_t * d_m
        d_s[...] += ldm[:T] + ldm[T:]
        d_x = dot(ls.astype(BF), gg, 0, 0)
        car = jnp.concatenate(tall(ca, 2))
        tow = jnp.concatenate(tall(ca, 3))
        c_u = car * dot(gg, start_b, 1, 0)
        d_c[...] += c_u[:T] + c_u[T:]
        c_own = cown[...]
        c_two = jnp.concatenate([c_own, c_own])
        r = jnp.sum(ldm * s_two + c_u * c_two, axis=1, keepdims=True)
        t_v = tow * dot(xx, end_b, 1, 0)
        d_b[...] += t_v[:T] + t_v[T:]
        d_xe = dot(bown[...].astype(BF), end_b, 1, 1) * toward_w
        d_xt = d_x + d_xe
        prod = xown * d_xt
        q_a = jnp.sum(jnp.where(low, prod, 0.0), axis=1, keepdims=True)
        q_b = jnp.sum(jnp.where(low, 0.0, prod), axis=1, keepdims=True)
        ends = jnp.sum(xt * d_xe, axis=0, keepdims=True)
        inner = end_grad * start
        low_row = low[:1]
        through_a, through_b = (v[T - 1 :, :] for v in tall(ca, 2))
        last_a = jnp.sum(jnp.where(low_row, ends, 0.0), axis=1, keepdims=True) + through_a * jnp.sum(
            jnp.sum(inner[:HEAD], axis=0, keepdims=True), axis=1, keepdims=True
        )
        last_b = jnp.sum(jnp.where(low_row, 0.0, ends), axis=1, keepdims=True) + through_b * jnp.sum(
            jnp.sum(inner[HEAD:], axis=0, keepdims=True), axis=1, keepdims=True
        )
        dt_a, dt_b = tall(ca, 0)
        final = row[:, :1] == T - 1
        cum_ga = r[:T] - dt_a * q_a + jnp.where(final, last_a, 0.0)
        cum_gb = r[T:] - dt_b * q_b + jnp.where(final, last_b, 0.0)
        placed = jnp.where(
            lane == 0,
            q_a,
            jnp.where(
                lane == 1, q_b, jnp.where(lane == 32, cum_ga, jnp.where(lane == 33, cum_gb, 0.0))
            ),
        )
        acc[...] += pltpu.roll(placed, 2 * i, 1)
        d_pre = (dt_w * d_xt + jnp.where(low_row, skip_ref[2 * i], skip_ref[2 * i + 1]) * gy) * dsilu
        own = taps[3:4, :] * d_pre
        rim = jnp.zeros((8, 128), F32)
        for k in range(3):
            d = 3 - k
            z = pltpu.roll(taps[k : k + 1, :] * masks[k, 2 * T :] * d_pre, T - d, 0)
            own += jnp.where(row < T - d, z, 0.0)
            rim += jnp.where(row[T - 8 :] < T - d, 0.0, z[T - 8 :])
        dx_ref[:, at] = own.astype(BF)
        tail_ref[:, at] = own[T - 8 :]
        rim_ref[:, at] = rim
        return carry

    lax.fori_loop(0, pairs, pair, 0)

    ds = d_s[...]
    full_c = d_c[...] + dot(ds, bown[...], 1, 0, EXACT)
    full_b = d_b[...] + dot(ds, cown[...], 0, 0, EXACT)
    d_pre = jnp.concatenate([full_b, full_c], axis=1) * silu_bc[...]
    own = taps_b[3:4, :] * d_pre
    rim = jnp.zeros((8, 2 * STATE), F32)
    row2 = lax.broadcasted_iota(jnp.int32, (T, 2 * STATE), 0)
    for k in range(3):
        d = 3 - k
        z = pltpu.roll(taps_b[k : k + 1, :] * tap_masks[k][2 * T : 3 * T] * d_pre, T - d, 0)
        own += jnp.where(row2 < T - d, z, 0.0)
        rim += jnp.where(row2[T - 8 :] < T - d, 0.0, z[T - 8 :])
    dbc_ref[...] = own
    rimbc_ref[...] = rim
    total = acc[...]
    d_log = pltpu.roll(dot(tri, total, 0, 0, EXACT), 96, 1)
    raw = raw_ref[2]
    ddt_ref[...] = ((total - decay * d_log) * jax.nn.sigmoid(raw))[:, :32]


def ssm_scratch(T):
    vm = pltpu.VMEM
    return [
        vm((3, 3 * T, 128), F32), vm((T, T), F32), vm((T, T), F32), vm((T, 128), F32),
        vm((T, 128), F32), vm((128, T), F32), vm((2 * T, STATE), BF), vm((2 * T, STATE), BF),
        vm((T, STATE), F32), vm((T, STATE), F32), vm((T, 2 * STATE), F32),
        vm((T, T), F32), vm((T, STATE), F32), vm((T, STATE), F32), vm((T, 128), F32),
    ]


SMEM = pl.BlockSpec(memory_space=pltpu.SMEM)
VMEM = pl.BlockSpec(memory_space=pltpu.VMEM)
ANY = pl.BlockSpec(memory_space=pl.ANY)


def local_kernel(span_ref, *refs):
    setup = ssm_setup(refs[0].shape[0], lax.axis_index("ctx"), span_ref, *refs[22:24])
    ssm_body(setup, *refs)


def ssm(span, xs, gs, bcs, raw, decay, skip, tapx, tapb):
    T, W = xs[0].shape
    return pl.pallas_call(
        local_kernel,
        in_specs=[SMEM] + [VMEM] * 13 + [SMEM] + [VMEM] * 2,
        out_shape=(
            jax.ShapeDtypeStruct((T, W), BF),
            jax.ShapeDtypeStruct((8, W), F32),
            jax.ShapeDtypeStruct((8, W), F32),
            jax.ShapeDtypeStruct((T, 2 * STATE), F32),
            jax.ShapeDtypeStruct((8, 2 * STATE), F32),
            jax.ShapeDtypeStruct((T, 32), F32),
        ),
        scratch_shapes=ssm_scratch(T),
        compiler_params=pltpu.CompilerParams(vmem_limit_bytes=40 << 20),
    )(span, *xs, *gs, *bcs, raw, decay, skip, tapx, tapb)


def fused_kernel(
    sizes, span_ref, skip_ref, hidden, w_bc, x_in, g_in, raw_in, decay_ref, tapx_ref, tapb_ref,
    dx_ref, du_ref, ddt_ref, dw_ref,
    hid_v, w_v, xbuf, gbuf, raws, bcs, part, part_in, tail, rim, rim_in, dbc, dbc_in,
    rimbc, rimbc_in, hid_slots, d_slots, local_sem, send, recv, *scratch
):
    n_ctx, n_fsdp, n_head = sizes
    c, f, h = (lax.axis_index(a) for a in ("ctx", "fsdp", "head"))
    T, W = x_in.shape
    half = hidden.shape[1]
    n_blocks = n_ctx * n_fsdp
    cols = half // n_blocks
    block = c * n_fsdp + f
    n_all = n_blocks * n_head
    me = block * n_head + h
    parts = 4
    step = W // parts

    barrier = pltpu.get_barrier_semaphore()
    for o in range(1, n_all):
        to = (me + o) % n_all
        pl.semaphore_signal(
            barrier, inc=1,
            device_id={"ctx": to // (n_fsdp * n_head), "fsdp": (to // n_head) % n_fsdp, "head": to % n_head},
            device_id_type=pl.DeviceIdType.MESH,
        )

    def remote(src, dst, k, **where):
        return pltpu.make_async_remote_copy(
            src_ref=src, dst_ref=dst, send_sem=send.at[k], recv_sem=recv.at[k],
            device_id=where, device_id_type=pl.DeviceIdType.MESH,
        )

    diagonal = f == h
    w_remote = remote(w_bc, w_v, 0, fsdp=h, head=f)
    w_local = pltpu.make_async_copy(w_bc, w_v, local_sem.at[0])
    loads = [
        pltpu.make_async_copy(hidden, hid_v, local_sem.at[1]),
        pltpu.make_async_copy(x_in, xbuf.at[2], local_sem.at[2]),
        pltpu.make_async_copy(g_in, gbuf.at[0], local_sem.at[3]),
        pltpu.make_async_copy(
            hidden.at[:, pl.ds(pl.multiple_of(block * cols, 128), cols)],
            hid_slots.at[0], local_sem.at[4],
        ),
    ]
    for load in loads:
        load.start()
    raws[2] = jnp.concatenate([raw_in[...]] * 4, axis=1)
    pl.semaphore_wait(barrier, n_all - 1)

    @pl.when(jnp.logical_not(diagonal))
    def _():
        w_remote.start()

    @pl.when(diagonal)
    def _():
        w_local.start()

    def span_of(p):
        return pl.ds(p * step, step)

    def hop1(p):
        return (
            remote(x_in.at[:, span_of(p)], xbuf.at[1, :, span_of(p)], 1 + p, ctx=c + 1),
            remote(g_in.at[:, span_of(p)], gbuf.at[1, :, span_of(p)], 5 + p, ctx=c - 1),
        )

    def hop2(p):
        return (
            remote(xbuf.at[1, :, span_of(p)], xbuf.at[0, :, span_of(p)], 9 + p, ctx=c + 1),
            remote(gbuf.at[1, :, span_of(p)], gbuf.at[2, :, span_of(p)], 13 + p, ctx=c - 1),
        )

    def small(buf, base):
        return [remote(buf.at[2], buf.at[2 - d], base + n, ctx=c + d) for n, d in enumerate((1, 2, -1, -2))]

    def sends(d):
        return (c + d >= 0) & (c + d < n_ctx)

    def gets(d):
        return (c - d >= 0) & (c - d < n_ctx)

    offsets = (1, 2, -1, -2)
    raw_copies, bc_copies = small(raws, 17), small(bcs, 21)
    for copy, d in zip(raw_copies, offsets):
        pl.when(sends(d))(copy.start)
    for p in range(parts):
        for copy, d in zip(hop1(p), (1, -1)):
            pl.when(sends(d))(copy.start)

    for d in offsets:

        @pl.when(jnp.logical_not(gets(d)))
        def _(d=d):
            raws[2 - d] = jnp.zeros_like(raws[2])
            bcs[2 - d] = jnp.zeros((T, 2 * STATE), BF)
            if d > 0:
                xbuf[2 - d] = jnp.zeros((T, W), BF)
            else:
                gbuf[-d] = jnp.zeros((T, W), BF)

    setup = ssm_setup(T, c, span_ref, *scratch[:2])

    for p in range(parts):
        for one, two, d in zip(hop1(p), hop2(p), (1, -1)):
            pl.when(gets(d))(one.wait_recv)
            pl.when(gets(d) & sends(d))(two.start)
    for load in loads:
        load.wait()
    pl.when(jnp.logical_not(diagonal))(w_remote.wait_recv)
    pl.when(diagonal)(w_local.wait)

    total = jnp.zeros((T, 2 * STATE), F32)
    for k in range(0, half, 512):
        total += dot(hid_v[:, k : k + 512], w_v[k : k + 512, :], 1, 0)
    part[...] = total
    swap_part = remote(part, part_in, 25, head=1 - h)
    swap_part.start()
    swap_part.wait_recv()
    bcs[2] = (part[...] + part_in[...]).astype(BF)
    for copy, d in zip(bc_copies, offsets):
        pl.when(sends(d))(copy.start)

    def spread(src, slots, base):
        out = []
        for o in range(1, n_blocks):
            to = (block + o) % n_blocks
            out.append(remote(src(to), slots.at[o], base + o, ctx=to // n_fsdp, fsdp=to % n_fsdp))
        return out

    for copies in (raw_copies, bc_copies):
        for copy, d in zip(copies, offsets):
            pl.when(gets(d))(copy.wait_recv)
    for p in range(parts):
        for copy, d in zip(hop2(p), (2, -2)):
            pl.when(gets(d))(copy.wait_recv)
    hid_copies = spread(
        lambda to: hidden.at[:, pl.ds(pl.multiple_of(to * cols, 128), cols)], hid_slots, 31
    )
    for copy in hid_copies:
        copy.start()

    ssm_body(
        setup, xbuf.at[0], xbuf.at[1], xbuf.at[2], gbuf.at[0], gbuf.at[1], gbuf.at[2],
        *(bcs.at[j] for j in range(5)), raws, decay_ref, skip_ref, tapx_ref, tapb_ref,
        dx_ref, tail, rim, dbc, rimbc, ddt_ref, *scratch
    )

    swap_d = remote(dbc, dbc_in, 26, head=1 - h)
    rim_a = remote(rimbc, rimbc_in.at[0], 27, ctx=c - 1)
    rim_b = remote(rimbc, rimbc_in.at[1], 28, ctx=c - 1, head=1 - h)
    rim_x = remote(rim, rim_in, 29, ctx=c - 1)
    swap_d.start()
    for copy in (rim_a, rim_b, rim_x):
        pl.when(sends(-1))(copy.start)

    @pl.when(jnp.logical_not(gets(-1)))
    def _():
        rimbc_in[...] = jnp.zeros_like(rimbc_in)
        rim_in[...] = jnp.zeros_like(rim_in)

    swap_d.wait_recv()
    for copy in (rim_a, rim_b):
        pl.when(gets(-1))(copy.wait_recv)
    d_sum = dbc[...] + dbc_in[...]
    edge = d_sum[T - 8 :] + (rimbc_in[0] + rimbc_in[1])
    d_bc = jnp.concatenate([d_sum[: T - 8], edge]).astype(BF)
    d_slots[0] = d_bc
    d_copies = spread(lambda to: d_slots.at[0], d_slots, 31 + n_blocks)
    for copy in d_copies:
        copy.start()
    for k in range(0, half, 512):
        du_ref[:, k : k + 512] = dot(d_bc, w_v[k : k + 512, :], 1, 1).astype(BF)
    pl.when(gets(-1))(rim_x.wait_recv)
    dx_ref[T - 16 :, :] = jnp.concatenate(
        [dx_ref[T - 16 : T - 8, :].astype(F32), tail[...] + rim_in[...]]
    ).astype(BF)
    for copy in hid_copies + d_copies:
        copy.wait_recv()
    left = hid_slots[...].reshape(n_blocks * T, cols)
    right = d_slots[...].reshape(n_blocks * T, 2 * STATE)
    dw_ref[...] = dot(left, right, 0, 0)

    pl.when(jnp.logical_not(diagonal))(w_remote.wait_send)
    for p in range(parts):
        for one, two, d in zip(hop1(p), hop2(p), (1, -1)):
            pl.when(sends(d))(one.wait_send)
            pl.when(gets(d) & sends(d))(two.wait_send)
    for copies in (raw_copies, bc_copies):
        for copy, d in zip(copies, offsets):
            pl.when(sends(d))(copy.wait_send)
    swap_part.wait_send()
    swap_d.wait_send()
    for copy in (rim_a, rim_b, rim_x):
        pl.when(sends(-1))(copy.wait_send)
    for copy in hid_copies + d_copies:
        copy.wait_send()


def fused(sizes, span, skip, hidden, w_bc, x, g, raw, decay, tapx, tapb):
    T, W = x.shape
    half = hidden.shape[1]
    n_blocks = sizes[0] * sizes[1]
    cols = half // n_blocks
    vm = pltpu.VMEM
    n_sem = 31 + 2 * n_blocks
    return pl.pallas_call(
        lambda *refs: fused_kernel(sizes, *refs),
        in_specs=[SMEM, SMEM, ANY, ANY, ANY, ANY, VMEM, VMEM, VMEM, VMEM],
        out_specs=[VMEM] * 4,
        out_shape=(
            jax.ShapeDtypeStruct((T, W), BF),
            jax.ShapeDtypeStruct((T, half), BF),
            jax.ShapeDtypeStruct((T, 32), F32),
            jax.ShapeDtypeStruct((cols, 2 * STATE), F32),
        ),
        scratch_shapes=[
            vm((T, half), BF), vm((half, 2 * STATE), BF), vm((3, T, W), BF), vm((3, T, W), BF),
            vm((5, T, 128), F32), vm((5, T, 2 * STATE), BF),
            vm((T, 2 * STATE), F32), vm((T, 2 * STATE), F32),
            vm((8, W), F32), vm((8, W), F32), vm((8, W), F32),
            vm((T, 2 * STATE), F32), vm((T, 2 * STATE), F32),
            vm((8, 2 * STATE), F32), vm((2, 8, 2 * STATE), F32),
            vm((n_blocks, T, cols), BF), vm((n_blocks, T, 2 * STATE), BF),
            pltpu.SemaphoreType.DMA((5,)),
            pltpu.SemaphoreType.DMA((n_sem,)),
            pltpu.SemaphoreType.DMA((n_sem,)),
        ] + ssm_scratch(T),
        compiler_params=pltpu.CompilerParams(
            vmem_limit_bytes=48 << 20, collective_id=0, has_side_effects=True
        ),
    )(span, skip, hidden, w_bc, x, g, raw, decay, tapx, tapb)


def on_device(
    hidden_in, w_bc, x_in, dt_raw, decay_rate, conv_x, conv_bc, skip_gain, span_len, grad_y
):
    T = x_in.shape[1]
    hidden = hidden_in[0]
    half_width = hidden.shape[1]
    n_ctx, n_fsdp, n_head = (lax.axis_size(a) for a in ("ctx", "fsdp", "head"))
    n_blocks = n_ctx * n_fsdp
    assert T * 2 == MOST and dt_raw.shape[2] == 32
    x0, g0, raw0 = x_in[0], grad_y[0], dt_raw[0]
    decay = decay_rate[None, :]
    if n_fsdp == 2 and n_head == 2 and (half_width // n_blocks) % 128 == 0:
        dx, du, ddt, dw = fused(
            (n_ctx, n_fsdp, n_head), span_len, skip_gain, hidden, w_bc, x0, g0, raw0, decay,
            conv_x, conv_bc,
        )
        return (dx[None], du[None], ddt[None], dw[None])
    w_full = lax.all_gather(w_bc, "fsdp", axis=0, tiled=True)
    w_half = lax.dynamic_slice_in_dim(w_full, lax.axis_index("head") * half_width, half_width, 0)

    def around(v):
        return [shifted(v, "ctx", d) for d in (2, 1)] + [v] + [shifted(v, "ctx", -d) for d in (1, 2)]

    raw = jnp.tile(jnp.stack(around(raw0)), (1, 1, 4))
    x2, x1 = shifted(x0, "ctx", 2), shifted(x0, "ctx", 1)
    g1, g2 = shifted(g0, "ctx", -1), shifted(g0, "ctx", -2)
    swap = [(i, (i + 1) % n_head) for i in range(n_head)]
    partial_bc = jnp.dot(hidden, w_half, preferred_element_type=F32)
    bc_pre = (partial_bc + lax.ppermute(partial_bc, "head", swap)).astype(BF)
    blocks = hidden.reshape(T, n_blocks, half_width // n_blocks).transpose(1, 0, 2)
    hidden_all = lax.all_to_all(blocks, ("ctx", "fsdp"), 0, 0, tiled=True)
    dx, tail, rim, dbc, rimbc, ddt = ssm(
        span_len, (x2, x1, x0), (g0, g1, g2), around(bc_pre), raw, decay, skip_gain, conv_x, conv_bc
    )
    back = shifted(rim, "ctx", -1)
    grad_x = lax.dynamic_update_slice(dx, (tail + back).astype(BF), (T - 8, 0))
    mine = dbc + jnp.pad(shifted(rimbc, "ctx", -1), ((T - 8, 0), (0, 0)))
    d_bc = (mine + lax.ppermute(mine, "head", swap)).astype(BF)
    grad_u = lax.dot_general(
        d_bc, w_half, (((1,), (1,)), ((), ())), preferred_element_type=F32
    ).astype(BF)
    d_all = lax.all_gather(d_bc, ("ctx", "fsdp"), axis=0)
    grad_w = lax.dot_general(
        hidden_all.reshape(n_blocks * T, -1), d_all.reshape(n_blocks * T, -1),
        (((0,), (0,)), ((), ())), preferred_element_type=F32,
    )
    return (grad_x[None], grad_u[None], ddt[None], grad_w[None])


def solution(mesh):
    return jax.shard_map(
        on_device,
        mesh=mesh,
        in_specs=(
            P(("groups", "fsdp"), "ctx", "head"),
            P("fsdp", None),
            P(("groups", "fsdp"), "ctx", "head"),
            P(("groups", "fsdp"), "ctx", "head"),
            P("head"),
            P(None, "head"),
            P(),
            P("head"),
            P(("groups", "fsdp"), None),
            P(("groups", "fsdp"), "ctx", "head"),
        ),
        out_specs=(
            P(("groups", "fsdp"), "ctx", "head"),
            P(("groups", "fsdp"), "ctx", "head"),
            P(("groups", "fsdp"), "ctx", "head"),
            P(("groups", "head"), ("ctx", "fsdp"), None),
        ),
        check_vma=False,
    )
```

```python
import jax
import jax.numpy as jnp
from jax import lax
from jax.experimental import pallas as pl
from jax.experimental.pallas import tpu as pltpu
from jax.sharding import PartitionSpec as P

STATE = 128
HEAD = 64
MOST = 256
W_PARTS = 4
PARTS = 4
BF = jnp.bfloat16
F32 = jnp.float32
EXACT = lax.Precision.HIGHEST


def shifted(block, axis, distance):
    devices = range(lax.axis_size(axis))
    route = [(i - distance, i) for i in devices if i - distance in devices]
    return lax.ppermute(block, axis, route)


def dot(a, b, ca, cb, precision=None):
    return lax.dot_general(
        a, b, (((ca,), (cb,)), ((), ())), precision=precision, preferred_element_type=F32
    )


def ssm_setup(T, c, span_ref, masks, bias_ref):
    spans = span_ref.shape[1]
    ends, total = [], 0
    for i in range(spans):
        total = total + span_ref[0, i]
        ends.append(total)

    def segment(p):
        count = sum((e <= p).astype(jnp.int32) if hasattr(p, "shape") and p.shape else jnp.where(e <= p, 1, 0) for e in ends)
        return jnp.where(p >= 0, count, -1)

    iota = lax.broadcasted_iota(jnp.int32, (T, 1), 0)
    taps, alive, last_same = [[], [], []], [], []
    for j in range(5):
        base = (c - 2 + j) * T
        pos = base + iota
        own = segment(pos)
        for k in range(3):
            taps[k].append((segment(pos - 3 + k) == own).astype(F32))
        alive.append((own == segment(base - 1)).astype(F32))
        last_same.append((own == segment(base + T - 1)).astype(F32))
    for k in range(3):
        masks[k] = jnp.broadcast_to(jnp.concatenate(taps[k][:3]), (3 * T, 128))
    row_pos = c * T + lax.broadcasted_iota(jnp.int32, (1, T), 1)
    same = segment(c * T + iota) == segment(row_pos)
    row = lax.broadcasted_iota(jnp.int32, (T, T), 0)
    lane = lax.broadcasted_iota(jnp.int32, (T, T), 1)
    bias_ref[...] = jnp.where(same & (row >= lane), 0.0, -1e30)
    return [jnp.concatenate(t) for t in taps], alive, last_same


def ssm_body(
    gate, setup, x2, x1, x0, g0, g1, g2, b2, b1, b0, b3, b4, raw_ref,
    decay_ref, skip_ref, tapx_ref, tapb_ref,
    dx_ref, tail_ref, rim_ref, dbc_ref, rimbc_ref, ddt_ref,
    masks, bias_ref, s_ref, cols_a, cols_b, cum_rows, bprev, cnext, bown, cown,
    silu_bc, d_s, d_b, d_c, acc,
):
    T = x0.shape[0]
    pairs = x0.shape[1] // 128
    lane = lax.broadcasted_iota(jnp.int32, (T, 128), 1)
    row = lax.broadcasted_iota(jnp.int32, (T, 128), 0)
    low = lane < HEAD
    group = lane // 32
    tap_masks, alive, last_same = setup
    tri = (row >= lane).astype(F32)
    decay = jnp.concatenate([decay_ref[...]] * 4, axis=1)
    dts, cums, carried, toward = [], [], [], []
    for j in range(5):
        raw = raw_ref[j]
        dt = jnp.maximum(raw, 0.0) + jnp.log1p(jnp.exp(-jnp.abs(raw)))
        cum = dot(tri, -dt * decay, 1, 0, EXACT)
        dts.append(dt)
        cums.append(cum)
        carried.append(jnp.exp(cum) * alive[j])
        toward.append(jnp.exp(cum[T - 1 :, :] - cum) * last_same[j])
    a1 = dts[1] * toward[1]
    a2 = dts[0] * toward[0] * carried[1][T - 1 :, :]
    c1 = carried[3]
    c2 = carried[4] * carried[3][T - 1 :, :]

    def packed(p, q, r, s):
        return jnp.where(group == 0, p, jnp.where(group == 1, q, jnp.where(group == 2, r, s)))

    cols_a[...] = packed(dts[2], cums[2], carried[2], toward[2])
    cols_b[...] = packed(a2, a1, c1, c2)
    cum_rows[...] = cums[2].T

    taps_b = tapb_ref[...]
    bc = jnp.concatenate([b2[...], b1[...], b0[...], b3[...], b4[...]]).astype(F32)
    pre_bc = taps_b[3:4, :] * bc
    for k in range(3):
        pre_bc += taps_b[k : k + 1, :] * pltpu.roll(bc, 3 - k, 0) * tap_masks[k]
    sig_bc = jax.nn.sigmoid(pre_bc)
    conv_bc = pre_bc * sig_bc
    own_sig = sig_bc[2 * T : 3 * T]
    silu_bc[...] = own_sig * (1.0 + pre_bc[2 * T : 3 * T] * (1.0 - own_sig))
    bprev[...] = conv_bc[: 2 * T, :STATE].astype(BF)
    cnext[...] = conv_bc[3 * T :, STATE:].astype(BF)
    bown[...] = conv_bc[2 * T : 3 * T, :STATE]
    cown[...] = conv_bc[2 * T : 3 * T, STATE:]
    s_ref[...] = dot(cown[...], bown[...], 1, 1, EXACT)
    d_s[...] = jnp.zeros_like(d_s)
    d_b[...] = jnp.zeros_like(d_b)
    d_c[...] = jnp.zeros_like(d_c)
    acc[...] = jnp.zeros_like(acc)

    def pair(i, carry):
        at = pl.ds(pl.multiple_of(i * 128, 128), 128)
        ca = pltpu.roll(cols_a[...], (128 - 2 * i) % 128, 1)
        cb = pltpu.roll(cols_b[...], (128 - 2 * i) % 128, 1)

        def wide(c, q):
            return jnp.where(low, c[:, 32 * q : 32 * q + 1], c[:, 32 * q + 1 : 32 * q + 2])

        def tall(c, q):
            return c[:, 32 * q : 32 * q + 1], c[:, 32 * q + 1 : 32 * q + 2]

        taps = tapx_ref[:, at]
        xe = jnp.concatenate([x2[:, at], x1[:, at], x0[:, at]]).astype(F32)
        pre = taps[3:4, :] * xe
        for k in range(3):
            pre += taps[k : k + 1, :] * pltpu.roll(xe, 3 - k, 0) * masks[k]
        sig = jax.nn.sigmoid(pre)
        xc = pre * sig
        xown = xc[2 * T :]
        sown = sig[2 * T :]
        dsilu = sown * (1.0 + pre[2 * T :] * (1.0 - sown))
        dt_w = wide(ca, 0)
        toward_w = wide(ca, 3)
        xw = jnp.concatenate([xc[:T] * wide(cb, 0), xc[T : 2 * T] * wide(cb, 1)]).astype(BF)
        start = dot(xw, bprev[...], 0, 0)
        gw = jnp.concatenate(
            [g1[:, at].astype(F32) * wide(cb, 2), g2[:, at].astype(F32) * wide(cb, 3)]
        ).astype(BF)
        end_grad = dot(gw, cnext[...], 0, 0)
        start_b = start.astype(BF)
        end_b = end_grad.astype(BF)
        gy = g0[:, at].astype(F32)
        gg = jnp.concatenate([jnp.where(low, gy, 0.0), jnp.where(low, 0.0, gy)]).astype(BF)
        xt = xown * dt_w
        xt_b = xt.astype(BF)
        xx = jnp.concatenate([jnp.where(low, xt, 0.0), jnp.where(low, 0.0, xt)]).astype(BF)
        d_m = dot(gg, xt_b, 1, 1)
        cum_a, cum_b = tall(ca, 1)
        bias = bias_ref[...]
        decay_t = jnp.concatenate(
            [
                jnp.exp(cum_a - cum_rows[pl.ds(2 * i, 1), :] + bias),
                jnp.exp(cum_b - cum_rows[pl.ds(2 * i + 1, 1), :] + bias),
            ]
        )
        s_all = s_ref[...]
        s_two = jnp.concatenate([s_all, s_all])
        ls = decay_t * s_two
        ldm = decay_t * d_m
        d_s[...] += ldm[:T] + ldm[T:]
        d_x = dot(ls.astype(BF), gg, 0, 0)
        car = jnp.concatenate(tall(ca, 2))
        tow = jnp.concatenate(tall(ca, 3))
        c_u = car * dot(gg, start_b, 1, 0)
        d_c[...] += c_u[:T] + c_u[T:]
        c_own = cown[...]
        c_two = jnp.concatenate([c_own, c_own])
        r = jnp.sum(ldm * s_two + c_u * c_two, axis=1, keepdims=True)
        t_v = tow * dot(xx, end_b, 1, 0)
        d_b[...] += t_v[:T] + t_v[T:]
        d_xe = dot(bown[...].astype(BF), end_b, 1, 1) * toward_w
        d_xt = d_x + d_xe
        prod = xown * d_xt
        q_a = jnp.sum(jnp.where(low, prod, 0.0), axis=1, keepdims=True)
        q_b = jnp.sum(jnp.where(low, 0.0, prod), axis=1, keepdims=True)
        ends = jnp.sum(xt * d_xe, axis=0, keepdims=True)
        inner = end_grad * start
        low_row = low[:1]
        through_a, through_b = (v[T - 1 :, :] for v in tall(ca, 2))
        last_a = jnp.sum(jnp.where(low_row, ends, 0.0), axis=1, keepdims=True) + through_a * jnp.sum(
            jnp.sum(inner[:HEAD], axis=0, keepdims=True), axis=1, keepdims=True
        )
        last_b = jnp.sum(jnp.where(low_row, 0.0, ends), axis=1, keepdims=True) + through_b * jnp.sum(
            jnp.sum(inner[HEAD:], axis=0, keepdims=True), axis=1, keepdims=True
        )
        dt_a, dt_b = tall(ca, 0)
        final = row[:, :1] == T - 1
        cum_ga = r[:T] - dt_a * q_a + jnp.where(final, last_a, 0.0)
        cum_gb = r[T:] - dt_b * q_b + jnp.where(final, last_b, 0.0)
        placed = jnp.where(
            lane == 0,
            q_a,
            jnp.where(
                lane == 1, q_b, jnp.where(lane == 32, cum_ga, jnp.where(lane == 33, cum_gb, 0.0))
            ),
        )
        acc[...] += pltpu.roll(placed, 2 * i, 1)
        d_pre = (dt_w * d_xt + jnp.where(low_row, skip_ref[2 * i], skip_ref[2 * i + 1]) * gy) * dsilu
        own = taps[3:4, :] * d_pre
        rim = jnp.zeros((8, 128), F32)
        for k in range(3):
            d = 3 - k
            z = pltpu.roll(taps[k : k + 1, :] * masks[k, 2 * T :] * d_pre, T - d, 0)
            own += jnp.where(row < T - d, z, 0.0)
            rim += jnp.where(row[T - 8 :] < T - d, 0.0, z[T - 8 :])
        dx_ref[:, at] = own.astype(BF)
        tail_ref[:, at] = own[T - 8 :]
        rim_ref[:, at] = rim
        return carry

    def some(p, carry):
        gate(p)
        return lax.fori_loop(p * (pairs // PARTS), (p + 1) * (pairs // PARTS), pair, carry)

    lax.fori_loop(0, PARTS, some, 0)

    ds = d_s[...]
    full_c = d_c[...] + dot(ds, bown[...], 1, 0, EXACT)
    full_b = d_b[...] + dot(ds, cown[...], 0, 0, EXACT)
    d_pre = jnp.concatenate([full_b, full_c], axis=1) * silu_bc[...]
    own = taps_b[3:4, :] * d_pre
    rim = jnp.zeros((8, 2 * STATE), F32)
    row2 = lax.broadcasted_iota(jnp.int32, (T, 2 * STATE), 0)
    for k in range(3):
        d = 3 - k
        z = pltpu.roll(taps_b[k : k + 1, :] * tap_masks[k][2 * T : 3 * T] * d_pre, T - d, 0)
        own += jnp.where(row2 < T - d, z, 0.0)
        rim += jnp.where(row2[T - 8 :] < T - d, 0.0, z[T - 8 :])
    dbc_ref[...] = own
    rimbc_ref[...] = rim
    total = acc[...]
    d_log = pltpu.roll(dot(tri, total, 0, 0, EXACT), 96, 1)
    raw = raw_ref[2]
    ddt_ref[...] = ((total - decay * d_log) * jax.nn.sigmoid(raw)).T[:32]


def ssm_scratch(T):
    vm = pltpu.VMEM
    return [
        vm((3, 3 * T, 128), F32), vm((T, T), F32), vm((T, T), F32), vm((T, 128), F32),
        vm((T, 128), F32), vm((128, T), F32), vm((2 * T, STATE), BF), vm((2 * T, STATE), BF),
        vm((T, STATE), F32), vm((T, STATE), F32), vm((T, 2 * STATE), F32),
        vm((T, T), F32), vm((T, STATE), F32), vm((T, STATE), F32), vm((T, 128), F32),
    ]


SMEM = pl.BlockSpec(memory_space=pltpu.SMEM)
VMEM = pl.BlockSpec(memory_space=pltpu.VMEM)
ANY = pl.BlockSpec(memory_space=pl.ANY)


def local_kernel(span_ref, *refs):
    setup = ssm_setup(refs[0].shape[0], lax.axis_index("ctx"), span_ref, *refs[22:24])
    ssm_body(lambda p: None, setup, *refs)


def ssm(span, xs, gs, bcs, raw, decay, skip, tapx, tapb):
    T, W = xs[0].shape
    return pl.pallas_call(
        local_kernel,
        in_specs=[SMEM] + [VMEM] * 13 + [SMEM] + [VMEM] * 2,
        out_shape=(
            jax.ShapeDtypeStruct((T, W), BF),
            jax.ShapeDtypeStruct((8, W), F32),
            jax.ShapeDtypeStruct((8, W), F32),
            jax.ShapeDtypeStruct((T, 2 * STATE), F32),
            jax.ShapeDtypeStruct((8, 2 * STATE), F32),
            jax.ShapeDtypeStruct((32, T), F32),
        ),
        scratch_shapes=ssm_scratch(T),
        compiler_params=pltpu.CompilerParams(vmem_limit_bytes=40 << 20),
    )(span, *xs, *gs, *bcs, raw, decay, skip, tapx, tapb)


def fused_kernel(
    sizes, span_any, skip_any, hidden, w_bc, x_in, g_in, raw_any, decay_any, tapx_any, tapb_any,
    dx_ref, du_ref, ddt_ref, dw_ref,
    span_ref, skip_ref, raw_in, decay_ref, tapx_ref, tapb_ref, hid_v, w_v, xbuf, gbuf, raws, bcs, part, part_in, tail, rim, rim_in, dbc, dbc_in,
    rimbc, rimbc_in, hid_slots, d_slots, local_sem, send, recv, *scratch
):
    n_ctx, n_fsdp, n_head, n_groups = sizes
    c, f, h = (lax.axis_index(a) for a in ("ctx", "fsdp", "head"))
    T, W = x_in.shape
    half = hidden.shape[1]
    n_blocks = n_ctx * n_fsdp
    cols = half // n_blocks
    block = c * n_fsdp + f
    n_all = n_blocks * n_head
    me = block * n_head + h
    parts = PARTS
    step = W // parts

    barrier = pltpu.get_barrier_semaphore()
    for o in range(1, n_all):
        to = (me + o) % n_all
        pl.semaphore_signal(
            barrier, inc=1,
            device_id={"ctx": to // (n_fsdp * n_head), "fsdp": (to // n_head) % n_fsdp, "head": to % n_head},
            device_id_type=pl.DeviceIdType.MESH,
        )

    pl.semaphore_signal(
        barrier, inc=1, device_id={"groups": 1 - lax.axis_index("groups")},
        device_id_type=pl.DeviceIdType.MESH,
    )

    def remote(src, dst, k, **where):
        return pltpu.make_async_remote_copy(
            src_ref=src, dst_ref=dst, send_sem=send.at[k], recv_sem=recv.at[k],
            device_id=where, device_id_type=pl.DeviceIdType.MESH,
        )

    diagonal = f == h
    y = lax.axis_index("groups")
    share = half // n_groups
    piece = share // W_PARTS
    base_sem = 31 + 2 * n_blocks

    def w_rows(owner, q):
        return pl.ds(pl.multiple_of(owner * share + q * piece, 128), piece)

    def w_hop(q):
        rows = w_rows(y, q)
        return remote(w_bc.at[rows], w_v.at[rows], base_sem + q, fsdp=h, head=f)

    def w_across(q, owner):
        rows = w_rows(owner, q)
        return remote(w_v.at[rows], w_v.at[rows], base_sem + W_PARTS + q, groups=1 - y)

    w_local = pltpu.make_async_copy(w_bc, w_v, local_sem.at[0])
    first = [
        pltpu.make_async_copy(src, dst, local_sem.at[5 + n])
        for n, (src, dst) in enumerate(
            (
                (raw_any, raw_in), (span_any, span_ref), (skip_any, skip_ref),
                (decay_any, decay_ref), (tapx_any, tapx_ref), (tapb_any, tapb_ref),
            )
        )
    ]
    for load in first:
        load.start()
    loads = [
        pltpu.make_async_copy(hidden, hid_v, local_sem.at[1]),
        pltpu.make_async_copy(x_in, xbuf.at[2], local_sem.at[2]),
        pltpu.make_async_copy(g_in, gbuf.at[0], local_sem.at[3]),
        pltpu.make_async_copy(
            hidden.at[:, pl.ds(pl.multiple_of(block * cols, 128), cols)],
            hid_slots.at[0], local_sem.at[4],
        ),
    ]
    for load in loads:
        load.start()
    pl.semaphore_wait(barrier, n_all)

    @pl.when(jnp.logical_not(diagonal))
    def _():
        for q in range(W_PARTS):
            w_hop(q).start()

    @pl.when(diagonal)
    def _():
        w_local.start()

    def span_of(p):
        return pl.ds(pl.multiple_of(p * step, 128), step)

    def hop1(p):
        return (
            remote(x_in.at[:, span_of(p)], xbuf.at[1, :, span_of(p)], 1 + p, ctx=c + 1),
            remote(g_in.at[:, span_of(p)], gbuf.at[1, :, span_of(p)], 5 + p, ctx=c - 1),
        )

    def hop2(p):
        return (
            remote(xbuf.at[1, :, span_of(p)], xbuf.at[0, :, span_of(p)], 9 + p, ctx=c + 1),
            remote(gbuf.at[1, :, span_of(p)], gbuf.at[2, :, span_of(p)], 13 + p, ctx=c - 1),
        )

    def small(buf, base):
        return [remote(buf.at[2], buf.at[2 - d], base + n, ctx=c + d) for n, d in enumerate((1, 2, -1, -2))]

    def sends(d):
        return (c + d >= 0) & (c + d < n_ctx)

    def gets(d):
        return (c - d >= 0) & (c - d < n_ctx)

    offsets = (1, 2, -1, -2)
    raw_copies, bc_copies = small(raws, 17), small(bcs, 21)
    for p in range(parts):
        for copy, d in zip(hop1(p), (1, -1)):
            pl.when(sends(d))(copy.start)
    for load in first:
        load.wait()
    raws[2] = jnp.concatenate([raw_in[...]] * 4, axis=0).T
    for copy, d in zip(raw_copies, offsets):
        pl.when(sends(d))(copy.start)

    for d in offsets:

        @pl.when(jnp.logical_not(gets(d)))
        def _(d=d):
            raws[2 - d] = jnp.zeros_like(raws[2])
            bcs[2 - d] = jnp.zeros((T, 2 * STATE), BF)
            if d > 0:
                xbuf[2 - d] = jnp.zeros((T, W), BF)
            else:
                gbuf[-d] = jnp.zeros((T, W), BF)

    setup = ssm_setup(T, c, span_ref, *scratch[:2])

    def forward(p):
        for one, two, d in zip(hop1(p), hop2(p), (1, -1)):
            pl.when(gets(d))(one.wait_recv)
            pl.when(gets(d) & sends(d))(two.start)

    forward(0)
    for load in loads:
        load.wait()

    @pl.when(jnp.logical_not(diagonal))
    def _():
        for q in range(W_PARTS):
            w_hop(q).wait_recv()
            if n_groups == 2:
                w_across(q, y).start()
        if n_groups == 2:
            for q in range(W_PARTS):
                w_across(q, 1 - y).wait_recv()

    pl.when(diagonal)(w_local.wait)

    total = jnp.zeros((T, 2 * STATE), F32)
    for k in range(0, half, 512):
        total += dot(hid_v[:, k : k + 512], w_v[k : k + 512, :], 1, 0)
    part[...] = total
    swap_part = remote(part, part_in, 25, head=1 - h)
    swap_part.start()
    swap_part.wait_recv()
    bcs[2] = (part[...] + part_in[...]).astype(BF)
    for copy, d in zip(bc_copies, offsets):
        pl.when(sends(d))(copy.start)
    for p in range(1, parts):
        forward(p)

    def spread(src, slots, base):
        out = []
        for o in range(1, n_blocks):
            to = (block + o) % n_blocks
            out.append(remote(src(to), slots.at[o], base + o, ctx=to // n_fsdp, fsdp=to % n_fsdp))
        return out

    for copies in (raw_copies, bc_copies):
        for copy, d in zip(copies, offsets):
            pl.when(gets(d))(copy.wait_recv)
    hid_copies = spread(
        lambda to: hidden.at[:, pl.ds(pl.multiple_of(to * cols, 128), cols)], hid_slots, 31
    )

    def gate(p):
        for copy, d in zip(hop2(p), (2, -2)):
            pl.when(gets(d))(copy.wait_recv)

        @pl.when(p == 1)
        def _():
            for copy in hid_copies:
                copy.start()

    ssm_body(
        gate, setup, xbuf.at[0], xbuf.at[1], xbuf.at[2], gbuf.at[0], gbuf.at[1], gbuf.at[2],
        *(bcs.at[j] for j in range(5)), raws, decay_ref, skip_ref, tapx_ref, tapb_ref,
        dx_ref, tail, rim, dbc, rimbc, ddt_ref, *scratch
    )

    swap_d = remote(dbc, dbc_in, 26, head=1 - h)
    rim_a = remote(rimbc, rimbc_in.at[0], 27, ctx=c - 1)
    rim_b = remote(rimbc, rimbc_in.at[1], 28, ctx=c - 1, head=1 - h)
    rim_x = remote(rim, rim_in, 29, ctx=c - 1)
    swap_d.start()
    for copy in (rim_a, rim_b, rim_x):
        pl.when(sends(-1))(copy.start)

    @pl.when(jnp.logical_not(gets(-1)))
    def _():
        rimbc_in[...] = jnp.zeros_like(rimbc_in)
        rim_in[...] = jnp.zeros_like(rim_in)

    swap_d.wait_recv()
    for copy in (rim_a, rim_b):
        pl.when(gets(-1))(copy.wait_recv)
    d_sum = dbc[...] + dbc_in[...]
    edge = d_sum[T - 8 :] + (rimbc_in[0] + rimbc_in[1])
    d_bc = jnp.concatenate([d_sum[: T - 8], edge]).astype(BF)
    d_slots[0] = d_bc
    d_copies = spread(lambda to: d_slots.at[0], d_slots, 31 + n_blocks)
    for copy in d_copies:
        copy.start()
    for k in range(0, half, 512):
        du_ref[:, k : k + 512] = dot(d_bc, w_v[k : k + 512, :], 1, 1).astype(BF)
    pl.when(gets(-1))(rim_x.wait_recv)
    dx_ref[T - 16 :, :] = jnp.concatenate(
        [dx_ref[T - 16 : T - 8, :].astype(F32), tail[...] + rim_in[...]]
    ).astype(BF)
    for copy in hid_copies + d_copies:
        copy.wait_recv()
    left = hid_slots[...].reshape(n_blocks * T, cols)
    right = d_slots[...].reshape(n_blocks * T, 2 * STATE)
    dw_ref[...] = dot(left, right, 0, 0)

    @pl.when(jnp.logical_not(diagonal))
    def _():
        for q in range(W_PARTS):
            w_hop(q).wait_send()
            if n_groups == 2:
                w_across(q, y).wait_send()

    for p in range(parts):
        for one, two, d in zip(hop1(p), hop2(p), (1, -1)):
            pl.when(sends(d))(one.wait_send)
            pl.when(gets(d) & sends(d))(two.wait_send)
    for copies in (raw_copies, bc_copies):
        for copy, d in zip(copies, offsets):
            pl.when(sends(d))(copy.wait_send)
    swap_part.wait_send()
    swap_d.wait_send()
    for copy in (rim_a, rim_b, rim_x):
        pl.when(sends(-1))(copy.wait_send)
    for copy in hid_copies + d_copies:
        copy.wait_send()


def fused(sizes, span, skip, hidden, w_bc, x, g, raw, decay, tapx, tapb):
    T, W = x.shape
    half = hidden.shape[1]
    n_blocks = sizes[0] * sizes[1]
    cols = half // n_blocks
    vm = pltpu.VMEM
    n_sem = 31 + 2 * n_blocks + 2 * W_PARTS
    return pl.pallas_call(
        lambda *refs: fused_kernel(sizes, *refs),
        in_specs=[ANY] * 10,
        out_specs=[VMEM] * 4,
        out_shape=(
            jax.ShapeDtypeStruct((T, W), BF),
            jax.ShapeDtypeStruct((T, half), BF),
            jax.ShapeDtypeStruct((32, T), F32),
            jax.ShapeDtypeStruct((cols, 2 * STATE), F32),
        ),
        scratch_shapes=[
            pltpu.SMEM(span.shape, jnp.int32), pltpu.SMEM(skip.shape, F32), vm(raw.shape, F32),
            vm(decay.shape, F32), vm(tapx.shape, F32), vm(tapb.shape, F32),
            vm((T, half), BF), vm((half, 2 * STATE), BF), vm((3, T, W), BF), vm((3, T, W), BF),
            vm((5, T, 128), F32), vm((5, T, 2 * STATE), BF),
            vm((T, 2 * STATE), F32), vm((T, 2 * STATE), F32),
            vm((8, W), F32), vm((8, W), F32), vm((8, W), F32),
            vm((T, 2 * STATE), F32), vm((T, 2 * STATE), F32),
            vm((8, 2 * STATE), F32), vm((2, 8, 2 * STATE), F32),
            vm((n_blocks, T, cols), BF), vm((n_blocks, T, 2 * STATE), BF),
            pltpu.SemaphoreType.DMA((15,)),
            pltpu.SemaphoreType.DMA((n_sem,)),
            pltpu.SemaphoreType.DMA((n_sem,)),
        ] + ssm_scratch(T),
        compiler_params=pltpu.CompilerParams(
            vmem_limit_bytes=62 << 20, collective_id=0, has_side_effects=True
        ),
    )(span, skip, hidden, w_bc, x, g, raw, decay, tapx, tapb)


def on_device(
    hidden_in, w_bc, x_in, dt_raw, decay_rate, conv_x, conv_bc, skip_gain, span_len, grad_y
):
    T = x_in.shape[1]
    hidden = hidden_in[0]
    half_width = hidden.shape[1]
    n_ctx, n_fsdp, n_head, n_groups = (
        lax.axis_size(a) for a in ("ctx", "fsdp", "head", "groups")
    )
    n_blocks = n_ctx * n_fsdp
    assert T * 2 == MOST and dt_raw.shape[2] == 32
    x0, g0, raw0 = x_in[0], grad_y[0], dt_raw[0]
    decay = decay_rate[None, :]
    if n_fsdp == 2 and n_head == 2 and n_groups == 2 and (half_width // n_blocks) % 128 == 0:
        dx, du, ddt, dw = fused(
            (n_ctx, n_fsdp, n_head, n_groups), span_len, skip_gain, hidden, w_bc, x0, g0, raw0.T, decay,
            conv_x, conv_bc,
        )
        return (dx[None], du[None], ddt.T[None], dw[None])
    w_full = lax.all_gather(w_bc, "fsdp", axis=0, tiled=True)
    w_half = lax.dynamic_slice_in_dim(w_full, lax.axis_index("head") * half_width, half_width, 0)

    def around(v):
        return [shifted(v, "ctx", d) for d in (2, 1)] + [v] + [shifted(v, "ctx", -d) for d in (1, 2)]

    raw = jnp.tile(jnp.stack(around(raw0)), (1, 1, 4))
    x2, x1 = shifted(x0, "ctx", 2), shifted(x0, "ctx", 1)
    g1, g2 = shifted(g0, "ctx", -1), shifted(g0, "ctx", -2)
    swap = [(i, (i + 1) % n_head) for i in range(n_head)]
    partial_bc = jnp.dot(hidden, w_half, preferred_element_type=F32)
    bc_pre = (partial_bc + lax.ppermute(partial_bc, "head", swap)).astype(BF)
    blocks = hidden.reshape(T, n_blocks, half_width // n_blocks).transpose(1, 0, 2)
    hidden_all = lax.all_to_all(blocks, ("ctx", "fsdp"), 0, 0, tiled=True)
    dx, tail, rim, dbc, rimbc, ddt = ssm(
        span_len, (x2, x1, x0), (g0, g1, g2), around(bc_pre), raw, decay, skip_gain, conv_x, conv_bc
    )
    back = shifted(rim, "ctx", -1)
    grad_x = lax.dynamic_update_slice(dx, (tail + back).astype(BF), (T - 8, 0))
    mine = dbc + jnp.pad(shifted(rimbc, "ctx", -1), ((T - 8, 0), (0, 0)))
    d_bc = (mine + lax.ppermute(mine, "head", swap)).astype(BF)
    grad_u = lax.dot_general(
        d_bc, w_half, (((1,), (1,)), ((), ())), preferred_element_type=F32
    ).astype(BF)
    d_all = lax.all_gather(d_bc, ("ctx", "fsdp"), axis=0)
    grad_w = lax.dot_general(
        hidden_all.reshape(n_blocks * T, -1), d_all.reshape(n_blocks * T, -1),
        (((0,), (0,)), ((), ())), preferred_element_type=F32,
    )
    return (grad_x[None], grad_u[None], ddt.T[None], grad_w[None])


def solution(mesh):
    return jax.shard_map(
        on_device,
        mesh=mesh,
        in_specs=(
            P(("groups", "fsdp"), "ctx", "head"),
            P("fsdp", None),
            P(("groups", "fsdp"), "ctx", "head"),
            P(("groups", "fsdp"), "ctx", "head"),
            P("head"),
            P(None, "head"),
            P(),
            P("head"),
            P(("groups", "fsdp"), None),
            P(("groups", "fsdp"), "ctx", "head"),
        ),
        out_specs=(
            P(("groups", "fsdp"), "ctx", "head"),
            P(("groups", "fsdp"), "ctx", "head"),
            P(("groups", "fsdp"), "ctx", "head"),
            P(("groups", "head"), ("ctx", "fsdp"), None),
        ),
        check_vma=False,
    )
```

```python
import jax
import jax.numpy as jnp
from jax import lax
from jax.experimental import pallas as pl
from jax.experimental.pallas import tpu as pltpu
from jax.sharding import PartitionSpec as P

STATE = 128
HEAD = 64
MOST = 256
W_PARTS = PARTS = 4
BF = jnp.bfloat16
F32 = jnp.float32
EXACT = lax.Precision.HIGHEST


def shifted(block, axis, distance):
    devices = range(lax.axis_size(axis))
    route = [(i - distance, i) for i in devices if i - distance in devices]
    return lax.ppermute(block, axis, route)


def dot(a, b, ca, cb, precision=None):
    return lax.dot_general(
        a, b, (((ca,), (cb,)), ((), ())), precision=precision, preferred_element_type=F32
    )


def ssm_setup(T, c, span_ref, masks, bias_ref):
    spans = span_ref.shape[1]
    ends, total = [], 0
    for i in range(spans):
        total = total + span_ref[0, i]
        ends.append(total)

    def segment(p):
        count = sum((e <= p).astype(jnp.int32) if hasattr(p, "shape") and p.shape else jnp.where(e <= p, 1, 0) for e in ends)
        return jnp.where(p >= 0, count, -1)

    iota = lax.broadcasted_iota(jnp.int32, (T, 1), 0)
    taps, alive, last_same = [[], [], []], [], []
    for j in range(5):
        base = (c - 2 + j) * T
        pos = base + iota
        own = segment(pos)
        for k in range(3):
            taps[k].append((segment(pos - 3 + k) == own).astype(F32))
        alive.append((own == segment(base - 1)).astype(F32))
        last_same.append((own == segment(base + T - 1)).astype(F32))
    for k in range(3):
        masks[k] = jnp.broadcast_to(jnp.concatenate(taps[k][:3]), (3 * T, 128))
    row_pos = c * T + lax.broadcasted_iota(jnp.int32, (1, T), 1)
    same = segment(c * T + iota) == segment(row_pos)
    row = lax.broadcasted_iota(jnp.int32, (T, T), 0)
    lane = lax.broadcasted_iota(jnp.int32, (T, T), 1)
    bias_ref[...] = jnp.where(same & (row >= lane), 0.0, -1e30)
    return [jnp.concatenate(t) for t in taps], alive, last_same


def ssm_body(
    gate, setup, x2, x1, x0, g0, g1, g2, b2, b1, b0, b3, b4, raw_ref,
    decay_ref, skip_ref, tapx_ref, tapb_ref,
    dx_ref, tail_ref, rim_ref, dbc_ref, rimbc_ref, ddt_ref,
    masks, bias_ref, s_ref, cols_a, cols_b, cum_rows, bprev, cnext, bown, cown,
    silu_bc, d_s, d_b, d_c, acc,
):
    T = x0.shape[0]
    pairs = x0.shape[1] // 128
    lane = lax.broadcasted_iota(jnp.int32, (T, 128), 1)
    row = lax.broadcasted_iota(jnp.int32, (T, 128), 0)
    low = lane < HEAD
    group = lane // 32
    tap_masks, alive, last_same = setup
    tri = (row >= lane).astype(F32)
    decay = jnp.concatenate([decay_ref[...]] * 4, axis=1)
    dts, cums, carried, toward = [], [], [], []
    for j in range(5):
        raw = raw_ref[j]
        dt = jnp.maximum(raw, 0.0) + jnp.log1p(jnp.exp(-jnp.abs(raw)))
        cum = dot(tri, -dt * decay, 1, 0, EXACT)
        dts.append(dt)
        cums.append(cum)
        carried.append(jnp.exp(cum) * alive[j])
        toward.append(jnp.exp(cum[T - 1 :, :] - cum) * last_same[j])
    a1 = dts[1] * toward[1]
    a2 = dts[0] * toward[0] * carried[1][T - 1 :, :]
    c1 = carried[3]
    c2 = carried[4] * carried[3][T - 1 :, :]

    def packed(p, q, r, s):
        return jnp.where(group == 0, p, jnp.where(group == 1, q, jnp.where(group == 2, r, s)))

    cols_a[...] = packed(dts[2], cums[2], carried[2], toward[2])
    cols_b[...] = packed(a2, a1, c1, c2)
    cum_rows[...] = cums[2].T

    taps_b = tapb_ref[...]
    bc = jnp.concatenate([b2[...], b1[...], b0[...], b3[...], b4[...]]).astype(F32)
    pre_bc = taps_b[3:4, :] * bc
    for k in range(3):
        pre_bc += taps_b[k : k + 1, :] * pltpu.roll(bc, 3 - k, 0) * tap_masks[k]
    sig_bc = jax.nn.sigmoid(pre_bc)
    conv_bc = pre_bc * sig_bc
    own_sig = sig_bc[2 * T : 3 * T]
    silu_bc[...] = own_sig * (1.0 + pre_bc[2 * T : 3 * T] * (1.0 - own_sig))
    bprev[...] = conv_bc[: 2 * T, :STATE].astype(BF)
    cnext[...] = conv_bc[3 * T :, STATE:].astype(BF)
    bown[...] = conv_bc[2 * T : 3 * T, :STATE]
    cown[...] = conv_bc[2 * T : 3 * T, STATE:]
    s_ref[...] = dot(cown[...], bown[...], 1, 1, EXACT)
    d_s[...] = jnp.zeros_like(d_s)
    d_b[...] = jnp.zeros_like(d_b)
    d_c[...] = jnp.zeros_like(d_c)
    acc[...] = jnp.zeros_like(acc)

    def pair(i, carry):
        at = pl.ds(pl.multiple_of(i * 128, 128), 128)
        ca = pltpu.roll(cols_a[...], (128 - 2 * i) % 128, 1)
        cb = pltpu.roll(cols_b[...], (128 - 2 * i) % 128, 1)

        def wide(c, q):
            return jnp.where(low, c[:, 32 * q : 32 * q + 1], c[:, 32 * q + 1 : 32 * q + 2])

        def tall(c, q):
            return c[:, 32 * q : 32 * q + 1], c[:, 32 * q + 1 : 32 * q + 2]

        taps = tapx_ref[:, at]
        xe = jnp.concatenate([x2[:, at], x1[:, at], x0[:, at]]).astype(F32)
        pre = taps[3:4, :] * xe
        for k in range(3):
            pre += taps[k : k + 1, :] * pltpu.roll(xe, 3 - k, 0) * masks[k]
        sig = jax.nn.sigmoid(pre)
        xc = pre * sig
        xown = xc[2 * T :]
        sown = sig[2 * T :]
        dsilu = sown * (1.0 + pre[2 * T :] * (1.0 - sown))
        dt_w = wide(ca, 0)
        toward_w = wide(ca, 3)
        xw = jnp.concatenate([xc[:T] * wide(cb, 0), xc[T : 2 * T] * wide(cb, 1)]).astype(BF)
        start = dot(xw, bprev[...], 0, 0)
        gw = jnp.concatenate(
            [g1[:, at].astype(F32) * wide(cb, 2), g2[:, at].astype(F32) * wide(cb, 3)]
        ).astype(BF)
        end_grad = dot(gw, cnext[...], 0, 0)
        start_b = start.astype(BF)
        end_b = end_grad.astype(BF)
        gy = g0[:, at].astype(F32)
        gg = jnp.concatenate([jnp.where(low, gy, 0.0), jnp.where(low, 0.0, gy)]).astype(BF)
        xt = xown * dt_w
        xt_b = xt.astype(BF)
        xx = jnp.concatenate([jnp.where(low, xt, 0.0), jnp.where(low, 0.0, xt)]).astype(BF)
        d_m = dot(gg, xt_b, 1, 1)
        cum_a, cum_b = tall(ca, 1)
        bias = bias_ref[...]
        decay_t = jnp.concatenate(
            [
                jnp.exp(cum_a - cum_rows[pl.ds(2 * i, 1), :] + bias),
                jnp.exp(cum_b - cum_rows[pl.ds(2 * i + 1, 1), :] + bias),
            ]
        )
        s_all = s_ref[...]
        s_two = jnp.concatenate([s_all, s_all])
        ls = decay_t * s_two
        ldm = decay_t * d_m
        d_s[...] += ldm[:T] + ldm[T:]
        d_x = dot(ls.astype(BF), gg, 0, 0)
        car = jnp.concatenate(tall(ca, 2))
        tow = jnp.concatenate(tall(ca, 3))
        c_u = car * dot(gg, start_b, 1, 0)
        d_c[...] += c_u[:T] + c_u[T:]
        c_own = cown[...]
        c_two = jnp.concatenate([c_own, c_own])
        r = jnp.sum(ldm * s_two + c_u * c_two, axis=1, keepdims=True)
        t_v = tow * dot(xx, end_b, 1, 0)
        d_b[...] += t_v[:T] + t_v[T:]
        d_xe = dot(bown[...].astype(BF), end_b, 1, 1) * toward_w
        d_xt = d_x + d_xe
        prod = xown * d_xt
        q_a = jnp.sum(jnp.where(low, prod, 0.0), axis=1, keepdims=True)
        q_b = jnp.sum(jnp.where(low, 0.0, prod), axis=1, keepdims=True)
        ends = jnp.sum(xt * d_xe, axis=0, keepdims=True)
        inner = end_grad * start
        low_row = low[:1]
        through_a, through_b = (v[T - 1 :, :] for v in tall(ca, 2))
        last_a = jnp.sum(jnp.where(low_row, ends, 0.0), axis=1, keepdims=True) + through_a * jnp.sum(
            jnp.sum(inner[:HEAD], axis=0, keepdims=True), axis=1, keepdims=True
        )
        last_b = jnp.sum(jnp.where(low_row, 0.0, ends), axis=1, keepdims=True) + through_b * jnp.sum(
            jnp.sum(inner[HEAD:], axis=0, keepdims=True), axis=1, keepdims=True
        )
        dt_a, dt_b = tall(ca, 0)
        final = row[:, :1] == T - 1
        cum_ga = r[:T] - dt_a * q_a + jnp.where(final, last_a, 0.0)
        cum_gb = r[T:] - dt_b * q_b + jnp.where(final, last_b, 0.0)
        placed = jnp.where(
            lane == 0,
            q_a,
            jnp.where(
                lane == 1, q_b, jnp.where(lane == 32, cum_ga, jnp.where(lane == 33, cum_gb, 0.0))
            ),
        )
        acc[...] += pltpu.roll(placed, 2 * i, 1)
        d_pre = (dt_w * d_xt + jnp.where(low_row, skip_ref[2 * i], skip_ref[2 * i + 1]) * gy) * dsilu
        own = taps[3:4, :] * d_pre
        rim = jnp.zeros((8, 128), F32)
        for k in range(3):
            d = 3 - k
            z = pltpu.roll(taps[k : k + 1, :] * masks[k, 2 * T :] * d_pre, T - d, 0)
            own += jnp.where(row < T - d, z, 0.0)
            rim += jnp.where(row[T - 8 :] < T - d, 0.0, z[T - 8 :])
        dx_ref[:, at] = own.astype(BF)
        tail_ref[:, at] = own[T - 8 :]
        rim_ref[:, at] = rim
        return carry

    def some(p, carry):
        gate(p)
        return lax.fori_loop(p * (pairs // PARTS), (p + 1) * (pairs // PARTS), pair, carry)

    lax.fori_loop(0, PARTS, some, 0)

    ds = d_s[...]
    full_c = d_c[...] + dot(ds, bown[...], 1, 0, EXACT)
    full_b = d_b[...] + dot(ds, cown[...], 0, 0, EXACT)
    d_pre = jnp.concatenate([full_b, full_c], axis=1) * silu_bc[...]
    own = taps_b[3:4, :] * d_pre
    rim = jnp.zeros((8, 2 * STATE), F32)
    row2 = lax.broadcasted_iota(jnp.int32, (T, 2 * STATE), 0)
    for k in range(3):
        d = 3 - k
        z = pltpu.roll(taps_b[k : k + 1, :] * tap_masks[k][2 * T : 3 * T] * d_pre, T - d, 0)
        own += jnp.where(row2 < T - d, z, 0.0)
        rim += jnp.where(row2[T - 8 :] < T - d, 0.0, z[T - 8 :])
    dbc_ref[...] = own
    rimbc_ref[...] = rim
    total = acc[...]
    d_log = pltpu.roll(dot(tri, total, 0, 0, EXACT), 96, 1)
    raw = raw_ref[2]
    ddt_ref[...] = ((total - decay * d_log) * jax.nn.sigmoid(raw)).T[:32]


def ssm_scratch(T):
    vm = pltpu.VMEM
    return [
        vm((3, 3 * T, 128), F32), vm((T, T), F32), vm((T, T), F32), vm((T, 128), F32),
        vm((T, 128), F32), vm((128, T), F32), vm((2 * T, STATE), BF), vm((2 * T, STATE), BF),
        vm((T, STATE), F32), vm((T, STATE), F32), vm((T, 2 * STATE), F32),
        vm((T, T), F32), vm((T, STATE), F32), vm((T, STATE), F32), vm((T, 128), F32),
    ]


SMEM = pl.BlockSpec(memory_space=pltpu.SMEM)
VMEM = pl.BlockSpec(memory_space=pltpu.VMEM)
ANY = pl.BlockSpec(memory_space=pl.ANY)


def local_kernel(span_ref, *refs):
    setup = ssm_setup(refs[0].shape[0], lax.axis_index("ctx"), span_ref, *refs[22:24])
    ssm_body(lambda p: None, setup, *refs)


def ssm(span, xs, gs, bcs, raw, decay, skip, tapx, tapb):
    T, W = xs[0].shape
    return pl.pallas_call(
        local_kernel,
        in_specs=[SMEM] + [VMEM] * 13 + [SMEM] + [VMEM] * 2,
        out_shape=(
            jax.ShapeDtypeStruct((T, W), BF),
            jax.ShapeDtypeStruct((8, W), F32),
            jax.ShapeDtypeStruct((8, W), F32),
            jax.ShapeDtypeStruct((T, 2 * STATE), F32),
            jax.ShapeDtypeStruct((8, 2 * STATE), F32),
            jax.ShapeDtypeStruct((32, T), F32),
        ),
        scratch_shapes=ssm_scratch(T),
        compiler_params=pltpu.CompilerParams(vmem_limit_bytes=40 << 20),
    )(span, *xs, *gs, *bcs, raw, decay, skip, tapx, tapb)


def fused_kernel(
    sizes, span_any, skip_any, hidden, w_bc, x_in, g_in, raw_any, decay_any, tapx_any, tapb_any,
    dx_ref, du_ref, ddt_ref, dw_ref,
    span_ref, skip_ref, raw_in, decay_ref, tapx_ref, tapb_ref, hid_v, w_v, xbuf, gbuf, raws, bcs, part, part_in, tail, rim, rim_in, dbc, dbc_in,
    rimbc, rimbc_in, hid_slots, d_slots, local_sem, send, recv, *scratch
):
    n_ctx, n_fsdp, n_head, n_groups = sizes
    c, f, h = (lax.axis_index(a) for a in ("ctx", "fsdp", "head"))
    T, W = x_in.shape
    half = hidden.shape[1]
    n_blocks = n_ctx * n_fsdp
    cols = half // n_blocks
    block = c * n_fsdp + f
    n_all = n_blocks * n_head
    me = block * n_head + h
    parts = PARTS
    step = W // parts

    barrier = pltpu.get_barrier_semaphore()
    for o in range(1, n_all):
        to = (me + o) % n_all
        pl.semaphore_signal(
            barrier, inc=1,
            device_id={"ctx": to // (n_fsdp * n_head), "fsdp": (to // n_head) % n_fsdp, "head": to % n_head},
            device_id_type=pl.DeviceIdType.MESH,
        )

    pl.semaphore_signal(
        barrier, inc=1, device_id={"groups": 1 - lax.axis_index("groups")},
        device_id_type=pl.DeviceIdType.MESH,
    )

    def remote(src, dst, k, **where):
        return pltpu.make_async_remote_copy(
            src_ref=src, dst_ref=dst, send_sem=send.at[k], recv_sem=recv.at[k],
            device_id=where, device_id_type=pl.DeviceIdType.MESH,
        )

    diagonal = f == h
    y = lax.axis_index("groups")
    share = half // n_groups
    piece = share // W_PARTS
    base_sem = 31 + 2 * n_blocks

    def w_rows(owner, q):
        return pl.ds(pl.multiple_of(owner * share + q * piece, 128), piece)

    def w_hop(q):
        rows = w_rows(y, q)
        return remote(w_bc.at[rows], w_v.at[rows], base_sem + q, fsdp=h, head=f)

    def w_across(q, owner):
        rows = w_rows(owner, q)
        return remote(w_v.at[rows], w_v.at[rows], base_sem + W_PARTS + q, groups=1 - y)

    w_local = pltpu.make_async_copy(w_bc, w_v, local_sem.at[0])
    first = [
        pltpu.make_async_copy(src, dst, local_sem.at[5 + n])
        for n, (src, dst) in enumerate(
            (
                (raw_any, raw_in), (span_any, span_ref), (skip_any, skip_ref),
                (decay_any, decay_ref), (tapx_any, tapx_ref), (tapb_any, tapb_ref),
            )
        )
    ]
    for load in first:
        load.start()
    loads = [
        pltpu.make_async_copy(hidden, hid_v, local_sem.at[1]),
        pltpu.make_async_copy(x_in, xbuf.at[2], local_sem.at[2]),
        pltpu.make_async_copy(g_in, gbuf.at[0], local_sem.at[3]),
        pltpu.make_async_copy(
            hidden.at[:, pl.ds(pl.multiple_of(block * cols, 128), cols)],
            hid_slots.at[0], local_sem.at[4],
        ),
    ]
    for load in loads:
        load.start()
    pl.semaphore_wait(barrier, n_all)

    @pl.when(jnp.logical_not(diagonal))
    def _():
        for q in range(W_PARTS):
            w_hop(q).start()

    @pl.when(diagonal)
    def _():
        w_local.start()

    def span_of(p):
        return pl.ds(pl.multiple_of(p * step, 128), step)

    def hop1(p):
        return (
            remote(x_in.at[:, span_of(p)], xbuf.at[1, :, span_of(p)], 1 + p, ctx=c + 1),
            remote(g_in.at[:, span_of(p)], gbuf.at[1, :, span_of(p)], 5 + p, ctx=c - 1),
        )

    def hop2(p):
        return (
            remote(xbuf.at[1, :, span_of(p)], xbuf.at[0, :, span_of(p)], 9 + p, ctx=c + 1),
            remote(gbuf.at[1, :, span_of(p)], gbuf.at[2, :, span_of(p)], 13 + p, ctx=c - 1),
        )

    def small(buf, base):
        return [remote(buf.at[2], buf.at[2 - d], base + n, ctx=c + d) for n, d in enumerate((1, 2, -1, -2))]

    def sends(d):
        return (c + d >= 0) & (c + d < n_ctx)

    def gets(d):
        return (c - d >= 0) & (c - d < n_ctx)

    offsets = (1, 2, -1, -2)
    raw_copies, bc_copies = small(raws, 17), small(bcs, 21)
    for p in range(parts):
        for copy, d in zip(hop1(p), (1, -1)):
            pl.when(sends(d))(copy.start)
    for load in first:
        load.wait()
    raws[2] = jnp.concatenate([raw_in[...]] * 4, axis=0).T
    for copy, d in zip(raw_copies, offsets):
        pl.when(sends(d))(copy.start)

    for d in offsets:

        @pl.when(jnp.logical_not(gets(d)))
        def _(d=d):
            raws[2 - d] = jnp.zeros_like(raws[2])
            bcs[2 - d] = jnp.zeros((T, 2 * STATE), BF)
            if d > 0:
                xbuf[2 - d] = jnp.zeros((T, W), BF)
            else:
                gbuf[-d] = jnp.zeros((T, W), BF)

    setup = ssm_setup(T, c, span_ref, *scratch[:2])

    def forward(p):
        for one, two, d in zip(hop1(p), hop2(p), (1, -1)):
            pl.when(gets(d))(one.wait_recv)
            pl.when(gets(d) & sends(d))(two.start)

    for q in range(parts):
        forward(q)

        @pl.when(jnp.logical_not(diagonal))
        def _(q=q):
            w_hop(q).wait_recv()
            w_across(q, y).start()

    for load in loads:
        load.wait()

    @pl.when(jnp.logical_not(diagonal))
    def _():
        if n_groups == 2:
            for q in range(W_PARTS):
                w_across(q, 1 - y).wait_recv()

    pl.when(diagonal)(w_local.wait)

    total = jnp.zeros((T, 2 * STATE), F32)
    for k in range(0, half, 512):
        total += dot(hid_v[:, k : k + 512], w_v[k : k + 512, :], 1, 0)
    part[...] = total
    swap_part = remote(part, part_in, 25, head=1 - h)
    swap_part.start()
    swap_part.wait_recv()
    bcs[2] = (part[...] + part_in[...]).astype(BF)
    for copy, d in zip(bc_copies, offsets):
        pl.when(sends(d))(copy.start)
    def spread(src, slots, base):
        out = []
        for o in range(1, n_blocks):
            to = (block + o) % n_blocks
            out.append(remote(src(to), slots.at[o], base + o, ctx=to // n_fsdp, fsdp=to % n_fsdp))
        return out

    for copies in (raw_copies, bc_copies):
        for copy, d in zip(copies, offsets):
            pl.when(gets(d))(copy.wait_recv)
    hid_copies = spread(
        lambda to: hidden.at[:, pl.ds(pl.multiple_of(to * cols, 128), cols)], hid_slots, 31
    )

    def gate(p):
        for copy, d in zip(hop2(p), (2, -2)):
            pl.when(gets(d))(copy.wait_recv)

    for copy in hid_copies:
        copy.start()
    ssm_body(
        gate, setup, xbuf.at[0], xbuf.at[1], xbuf.at[2], gbuf.at[0], gbuf.at[1], gbuf.at[2],
        *(bcs.at[j] for j in range(5)), raws, decay_ref, skip_ref, tapx_ref, tapb_ref,
        dx_ref, tail, rim, dbc, rimbc, ddt_ref, *scratch
    )

    swap_d = remote(dbc, dbc_in, 26, head=1 - h)
    rim_a = remote(rimbc, rimbc_in.at[0], 27, ctx=c - 1)
    rim_b = remote(rimbc, rimbc_in.at[1], 28, ctx=c - 1, head=1 - h)
    rim_x = remote(rim, rim_in, 29, ctx=c - 1)
    swap_d.start()
    for copy in (rim_a, rim_b, rim_x):
        pl.when(sends(-1))(copy.start)

    @pl.when(jnp.logical_not(gets(-1)))
    def _():
        rimbc_in[...] = jnp.zeros_like(rimbc_in)
        rim_in[...] = jnp.zeros_like(rim_in)

    swap_d.wait_recv()
    for copy in (rim_a, rim_b):
        pl.when(gets(-1))(copy.wait_recv)
    d_sum = dbc[...] + dbc_in[...]
    edge = d_sum[T - 8 :] + (rimbc_in[0] + rimbc_in[1])
    d_bc = jnp.concatenate([d_sum[: T - 8], edge]).astype(BF)
    d_slots[0] = d_bc
    d_copies = spread(lambda to: d_slots.at[0], d_slots, 31 + n_blocks)
    for copy in d_copies:
        copy.start()
    for k in range(0, half, 512):
        du_ref[:, k : k + 512] = dot(d_bc, w_v[k : k + 512, :], 1, 1).astype(BF)
    pl.when(gets(-1))(rim_x.wait_recv)
    dx_ref[T - 16 :, :] = jnp.concatenate(
        [dx_ref[T - 16 : T - 8, :].astype(F32), tail[...] + rim_in[...]]
    ).astype(BF)
    for copy in hid_copies + d_copies:
        copy.wait_recv()
    left = hid_slots[...].reshape(n_blocks * T, cols)
    right = d_slots[...].reshape(n_blocks * T, 2 * STATE)
    dw_ref[...] = dot(left, right, 0, 0)

    @pl.when(jnp.logical_not(diagonal))
    def _():
        for q in range(W_PARTS):
            w_hop(q).wait_send()
            if n_groups == 2:
                w_across(q, y).wait_send()

    for p in range(parts):
        for one, two, d in zip(hop1(p), hop2(p), (1, -1)):
            pl.when(sends(d))(one.wait_send)
            pl.when(gets(d) & sends(d))(two.wait_send)
    for copies in (raw_copies, bc_copies):
        for copy, d in zip(copies, offsets):
            pl.when(sends(d))(copy.wait_send)
    swap_part.wait_send()
    swap_d.wait_send()
    for copy in (rim_a, rim_b, rim_x):
        pl.when(sends(-1))(copy.wait_send)
    for copy in hid_copies + d_copies:
        copy.wait_send()


def fused(sizes, span, skip, hidden, w_bc, x, g, raw, decay, tapx, tapb):
    T, W = x.shape
    half = hidden.shape[1]
    n_blocks = sizes[0] * sizes[1]
    cols = half // n_blocks
    vm = pltpu.VMEM
    n_sem = 31 + 2 * n_blocks + 2 * W_PARTS
    return pl.pallas_call(
        lambda *refs: fused_kernel(sizes, *refs),
        in_specs=[ANY] * 10,
        out_specs=[VMEM] * 4,
        out_shape=(
            jax.ShapeDtypeStruct((T, W), BF),
            jax.ShapeDtypeStruct((T, half), BF),
            jax.ShapeDtypeStruct((32, T), F32),
            jax.ShapeDtypeStruct((cols, 2 * STATE), F32),
        ),
        scratch_shapes=[
            pltpu.SMEM(span.shape, jnp.int32), pltpu.SMEM(skip.shape, F32), vm(raw.shape, F32),
            vm(decay.shape, F32), vm(tapx.shape, F32), vm(tapb.shape, F32),
            vm((T, half), BF), vm((half, 2 * STATE), BF), vm((3, T, W), BF), vm((3, T, W), BF),
            vm((5, T, 128), F32), vm((5, T, 2 * STATE), BF),
            vm((T, 2 * STATE), F32), vm((T, 2 * STATE), F32),
            vm((8, W), F32), vm((8, W), F32), vm((8, W), F32),
            vm((T, 2 * STATE), F32), vm((T, 2 * STATE), F32),
            vm((8, 2 * STATE), F32), vm((2, 8, 2 * STATE), F32),
            vm((n_blocks, T, cols), BF), vm((n_blocks, T, 2 * STATE), BF),
            pltpu.SemaphoreType.DMA((15,)),
            pltpu.SemaphoreType.DMA((n_sem,)),
            pltpu.SemaphoreType.DMA((n_sem,)),
        ] + ssm_scratch(T),
        compiler_params=pltpu.CompilerParams(
            vmem_limit_bytes=62 << 20, collective_id=0, has_side_effects=True
        ),
    )(span, skip, hidden, w_bc, x, g, raw, decay, tapx, tapb)


def on_device(
    hidden_in, w_bc, x_in, dt_raw, decay_rate, conv_x, conv_bc, skip_gain, span_len, grad_y
):
    T = x_in.shape[1]
    hidden = hidden_in[0]
    half_width = hidden.shape[1]
    n_ctx, n_fsdp, n_head, n_groups = (
        lax.axis_size(a) for a in ("ctx", "fsdp", "head", "groups")
    )
    n_blocks = n_ctx * n_fsdp
    assert T * 2 == MOST and dt_raw.shape[2] == 32
    x0, g0, raw0 = x_in[0], grad_y[0], dt_raw[0]
    decay = decay_rate[None, :]
    if n_fsdp == 2 and n_head == 2 and n_groups == 2 and (half_width // n_blocks) % 128 == 0:
        dx, du, ddt, dw = fused(
            (n_ctx, n_fsdp, n_head, n_groups), span_len, skip_gain, hidden, w_bc, x0, g0, raw0.T, decay,
            conv_x, conv_bc,
        )
        return (dx[None], du[None], ddt.T[None], dw[None])
    w_full = lax.all_gather(w_bc, "fsdp", axis=0, tiled=True)
    w_half = lax.dynamic_slice_in_dim(w_full, lax.axis_index("head") * half_width, half_width, 0)

    def around(v):
        return [shifted(v, "ctx", d) for d in (2, 1)] + [v] + [shifted(v, "ctx", -d) for d in (1, 2)]

    raw = jnp.tile(jnp.stack(around(raw0)), (1, 1, 4))
    x2, x1 = shifted(x0, "ctx", 2), shifted(x0, "ctx", 1)
    g1, g2 = shifted(g0, "ctx", -1), shifted(g0, "ctx", -2)
    swap = [(i, (i + 1) % n_head) for i in range(n_head)]
    partial_bc = jnp.dot(hidden, w_half, preferred_element_type=F32)
    bc_pre = (partial_bc + lax.ppermute(partial_bc, "head", swap)).astype(BF)
    blocks = hidden.reshape(T, n_blocks, half_width // n_blocks).transpose(1, 0, 2)
    hidden_all = lax.all_to_all(blocks, ("ctx", "fsdp"), 0, 0, tiled=True)
    dx, tail, rim, dbc, rimbc, ddt = ssm(
        span_len, (x2, x1, x0), (g0, g1, g2), around(bc_pre), raw, decay, skip_gain, conv_x, conv_bc
    )
    back = shifted(rim, "ctx", -1)
    grad_x = lax.dynamic_update_slice(dx, (tail + back).astype(BF), (T - 8, 0))
    mine = dbc + jnp.pad(shifted(rimbc, "ctx", -1), ((T - 8, 0), (0, 0)))
    d_bc = (mine + lax.ppermute(mine, "head", swap)).astype(BF)
    grad_u = lax.dot_general(
        d_bc, w_half, (((1,), (1,)), ((), ())), preferred_element_type=F32
    ).astype(BF)
    d_all = lax.all_gather(d_bc, ("ctx", "fsdp"), axis=0)
    grad_w = lax.dot_general(
        hidden_all.reshape(n_blocks * T, -1), d_all.reshape(n_blocks * T, -1),
        (((0,), (0,)), ((), ())), preferred_element_type=F32,
    )
    return (grad_x[None], grad_u[None], ddt.T[None], grad_w[None])


def solution(mesh):
    return jax.shard_map(
        on_device,
        mesh=mesh,
        in_specs=(
            P(("groups", "fsdp"), "ctx", "head"),
            P("fsdp", None),
            P(("groups", "fsdp"), "ctx", "head"),
            P(("groups", "fsdp"), "ctx", "head"),
            P("head"),
            P(None, "head"),
            P(),
            P("head"),
            P(("groups", "fsdp"), None),
            P(("groups", "fsdp"), "ctx", "head"),
        ),
        out_specs=(
            P(("groups", "fsdp"), "ctx", "head"),
            P(("groups", "fsdp"), "ctx", "head"),
            P(("groups", "fsdp"), "ctx", "head"),
            P(("groups", "head"), ("ctx", "fsdp"), None),
        ),
        check_vma=False,
    )
```
